32 devices in a mesh: fsdp: 8 (over y, x, core), ep: 4 (over z).
Axes of the slice: x: 2, y: 2, z: 4, core: 2. Of those that a mesh axis runs over, the one named last changes fastest.
Arguments:
- tokens: bfloat16 [8192, 2048], P(('fsdp', 'ep')), may hold values from -6 to 6
- out_grad: bfloat16 [8192, 2048], P(('fsdp', 'ep')), may hold values from -4 to 4
- expert_ids: int32 [8192, 8], P(('fsdp', 'ep')), may hold values from 0 to 127, as said below
- gate_probs: bfloat16 [8192, 8], P(('fsdp', 'ep')), may hold values from 0.19921875 to 1
- w_gate: bfloat16 [2048, 4, 768], P('fsdp', 'ep'), may hold values from -0.125 to 0.125
- w_up: bfloat16 [2048, 4, 768], P('fsdp', 'ep'), may hold values from -0.125 to 0.125
- w_down: bfloat16 [2048, 4, 768], P('fsdp', 'ep'), may hold values from -0.21875 to 0.21875
Outputs:
- in_grad: bfloat16 [8192, 2048], P(('fsdp', 'ep'))
- gate_grad: bfloat16 [8192, 8], P(('fsdp', 'ep'))
- grad_gate: bfloat16 [2048, 4, 768], P('fsdp', 'ep')
- grad_up: bfloat16 [2048, 4, 768], P('fsdp', 'ep')
- grad_down: bfloat16 [2048, 4, 768], P('fsdp', 'ep')
The draws below stay inside these ranges and needn't reach their ends.
Inputs may be any that keep to these rules, and one draw needn't show every extreme that they name: `expert_ids`: each token names 8 different experts. Among the 256 tokens of one device each expert below 4 is named by at most 32 tokens; in each group of devices that share an index of fsdp, one expert below 4 is named by exactly 32 tokens of every device of the group.
All inputs are finite; a program needn't handle non-finite values.
Results may differ from the reference program's by a relative error of at most 0.014.
Values may be sent and summed in bfloat16 or wider, within the bound.
No kernel may reach another device: no remote copies, remote signals or barrier semaphores. Data moves between devices by JAX's collectives and lax.ppermute only.
A program may use at most 128 MiB of HBM per device.

```python
import jax
import jax.numpy as jnp
from jax import lax

D = 2048
FF = 768
EXPERTS = 128
TOPK = 8
TOK_DEV = 256
MOST = 32
WIN = 4
TOKENS = 8192
N_FSDP = 8
N_EP = 4


def draw_expert_ids(key, part):
    blocks = TOKENS // TOK_DEV
    per_column = (N_EP + TOPK - 1) // TOPK
    keys = jax.random.split(jax.random.fold_in(key, 7), 5)
    counts = jax.random.randint(keys[0], (blocks, N_EP), 0, MOST)
    hottest = jax.random.randint(keys[1], (blocks // N_EP,), 0, N_EP)
    hot_rows = jnp.repeat(hottest, N_EP)
    counts = jnp.where(jnp.arange(N_EP)[None, :] == hot_rows[:, None], MOST, counts)
    padded = jnp.concatenate([counts, jnp.zeros((blocks, per_column * TOPK - N_EP), jnp.int32)], axis=1)
    padded = padded.reshape(blocks, per_column, TOPK)
    ends = jnp.cumsum(padded, axis=1)
    starts = ends - padded
    scores = jax.random.randint(keys[2], (blocks, TOPK, TOK_DEV), 0, 1 << 20) * TOK_DEV + jnp.arange(TOK_DEV)[None, None, :]
    order = jnp.argsort(scores, axis=-1)
    ranks = jnp.argsort(order, axis=-1)
    inside = (ranks[:, None, :, :] >= starts[:, :, :, None]) & (ranks[:, None, :, :] < ends[:, :, :, None])
    numbers = jnp.arange(per_column)[:, None] * TOPK + jnp.arange(TOPK)[None, :]
    window_ids = jnp.sum(jnp.where(inside, numbers[None, :, :, None] + 1, 0), axis=1) - 1
    window_ids = jnp.swapaxes(window_ids, 1, 2)
    others = EXPERTS - N_EP
    offsets = jax.random.randint(keys[3], (blocks, TOK_DEV, 1), 0, others)
    filler = N_EP + (offsets + jnp.arange(TOPK)[None, None, :]) % others
    columns = jnp.where(window_ids >= 0, window_ids, filler)
    column_scores = jax.random.randint(keys[4], (blocks, TOK_DEV, TOPK), 0, 1 << 20) * TOPK + jnp.arange(TOPK)[None, None, :]
    shuffle = jnp.argsort(column_scores, axis=-1)
    result = jnp.take_along_axis(columns, shuffle, axis=-1)
    return result.reshape(TOKENS, TOPK).astype(jnp.int32)


def shard_levels(own_key, dims, cuts, low, high):
    def one(dim, shards_of):
        draws = jax.random.uniform(jax.random.fold_in(jax.random.fold_in(own_key, 6), dim), (shards_of,), jnp.float32, low / len(cuts), high / len(cuts))
        return jnp.repeat(jnp.exp(draws), dims[dim] // shards_of).reshape((-1,) + (1,) * (len(dims) - dim - 1))

    loudness = one(*cuts[0])
    for cut in cuts[1:]:
        loudness = loudness * one(*cut)
    return loudness


def noise(rng, extent, scale, reach, cuts=(), dtype=jnp.bfloat16):
    drawn = scale * jax.random.normal(rng, extent, jnp.float32)
    if cuts:
        drawn = drawn * shard_levels(rng, extent, cuts, -0.22, 0.18)
    return jnp.clip(drawn, -reach, reach).astype(dtype)


def setup_inputs(seed: int = 0) -> dict:
    arg_keys = jax.random.split(jax.random.key(seed), 8)
    tokens = noise(arg_keys[0], (TOKENS, D), 1.0, 6.0, ((0, 32),))
    out_grad = noise(arg_keys[1], (TOKENS, D), 0.5, 4.0, ((0, 32),))
    expert_ids = draw_expert_ids(jax.random.fold_in(arg_keys[7], 71), 0)
    gate_probs = jnp.clip(0.19921875 + 0.80078125 * jax.random.uniform(arg_keys[3], (TOKENS, TOPK), jnp.float32) ** shard_levels(arg_keys[3], (TOKENS, TOPK), ((0, 32),), -0.2, 0.2), 0.19921875, 1.0).astype(jnp.bfloat16)
    w_gate = noise(arg_keys[4], (D, WIN, FF), D ** -0.5, 0.125, ((0, 8), (1, 4)))
    w_up = noise(arg_keys[5], (D, WIN, FF), D ** -0.5, 0.125, ((0, 8), (1, 4)))
    w_down = noise(arg_keys[6], (D, WIN, FF), FF ** -0.5, 0.21875, ((0, 8), (1, 4)))
    return dict(tokens=tokens, out_grad=out_grad, expert_ids=expert_ids, gate_probs=gate_probs, w_gate=w_gate, w_up=w_up, w_down=w_down)


def expert_math(grad_rows, gate_rows, gate_pre, up_pre, back_proj):
    sigmoid_gate = jax.nn.sigmoid(gate_pre)
    silu_gate = gate_pre * sigmoid_gate
    activated = (silu_gate * up_pre).astype(jnp.bfloat16)
    pick_grad = jnp.sum(activated.astype(jnp.float32) * back_proj, axis=-1).astype(jnp.bfloat16)
    weight_col = gate_rows.astype(jnp.float32)[:, None]
    scaled_back = weight_col * back_proj
    gate_delta = (scaled_back * up_pre * sigmoid_gate * (1.0 + gate_pre * (1.0 - sigmoid_gate))).astype(jnp.bfloat16)
    up_delta = (scaled_back * silu_gate).astype(jnp.bfloat16)
    scaled_grad = (weight_col * grad_rows.astype(jnp.float32)).astype(jnp.bfloat16)
    return activated, pick_grad, gate_delta, up_delta, scaled_grad


def reference(tokens, out_grad, expert_ids, gate_probs, w_gate, w_up, w_down):
    group = N_EP * TOK_DEV
    rows_cap = N_EP * MOST

    def one_group(totals, pieces):
        group_tokens, group_grads, group_ids, group_gates = pieces

        def one_expert(carry, expert):
            in_acc, pick_acc = carry
            matches = group_ids == expert
            chosen = jnp.any(matches, axis=1)
            gate_pick = jnp.sum(jnp.where(matches, group_gates.astype(jnp.float32), 0.0), axis=1)
            count = jnp.sum(chosen.astype(jnp.int32))
            positions = jnp.nonzero(chosen, size=rows_cap, fill_value=0)[0].astype(jnp.int32)
            valid = lax.iota(jnp.int32, rows_cap) < count
            row_tokens = jnp.where(valid[:, None], group_tokens[positions], jnp.zeros((), jnp.bfloat16))
            row_grads = jnp.where(valid[:, None], group_grads[positions], jnp.zeros((), jnp.bfloat16))
            row_gates = jnp.where(valid, gate_pick[positions], 0.0).astype(jnp.bfloat16)
            gate_weight = lax.dynamic_index_in_dim(w_gate, expert, 1, keepdims=False)
            up_weight = lax.dynamic_index_in_dim(w_up, expert, 1, keepdims=False)
            down_weight = lax.dynamic_index_in_dim(w_down, expert, 1, keepdims=False)
            gate_pre = jnp.dot(row_tokens, gate_weight, preferred_element_type=jnp.float32)
            up_pre = jnp.dot(row_tokens, up_weight, preferred_element_type=jnp.float32)
            back_proj = jnp.dot(row_grads, down_weight, preferred_element_type=jnp.float32)
            activated, pick_grad, gate_delta, up_delta, scaled_grad = expert_math(row_grads, row_gates, gate_pre, up_pre, back_proj)
            row_in = (jnp.dot(gate_delta, gate_weight.T, preferred_element_type=jnp.float32)
                      + jnp.dot(up_delta, up_weight.T, preferred_element_type=jnp.float32)).astype(jnp.bfloat16)
            in_part = jax.ops.segment_sum(jnp.where(valid[:, None], row_in.astype(jnp.float32), 0.0), positions, num_segments=group)
            pick_tokens = jax.ops.segment_sum(jnp.where(valid, pick_grad.astype(jnp.float32), 0.0), positions, num_segments=group)
            pick_part = jnp.where(matches, pick_tokens[:, None], 0.0)
            part_gate = jnp.dot(row_tokens.T, gate_delta, preferred_element_type=jnp.float32).astype(jnp.bfloat16)
            part_up = jnp.dot(row_tokens.T, up_delta, preferred_element_type=jnp.float32).astype(jnp.bfloat16)
            part_down = jnp.dot(scaled_grad.T, activated, preferred_element_type=jnp.float32).astype(jnp.bfloat16)
            return (in_acc + in_part, pick_acc + pick_part), (part_gate, part_up, part_down)

        start = (jnp.zeros((group, D), jnp.float32), jnp.zeros((group, TOPK), jnp.float32))
        (in_sum, pick_sum), parts = lax.scan(one_expert, start, lax.iota(jnp.int32, N_EP))
        totals = (totals[0] + parts[0].astype(jnp.float32), totals[1] + parts[1].astype(jnp.float32), totals[2] + parts[2].astype(jnp.float32))
        return totals, (in_sum.astype(jnp.bfloat16), pick_sum.astype(jnp.bfloat16))

    pieces = (tokens.reshape(N_FSDP, group, D), out_grad.reshape(N_FSDP, group, D),
              expert_ids.reshape(N_FSDP, group, TOPK), gate_probs.reshape(N_FSDP, group, TOPK))
    zeros_grad = jnp.zeros((N_EP, D, FF), jnp.float32)
    totals, outputs = lax.scan(one_group, (zeros_grad, zeros_grad, zeros_grad), pieces)
    grad_gate = jnp.transpose(totals[0], (1, 0, 2)).astype(jnp.bfloat16)
    grad_up = jnp.transpose(totals[1], (1, 0, 2)).astype(jnp.bfloat16)
    grad_down = jnp.transpose(totals[2], (1, 0, 2)).astype(jnp.bfloat16)
    return outputs[0].reshape(TOKENS, D), outputs[1].reshape(TOKENS, TOPK), grad_gate, grad_up, grad_down
```

```python
import functools

import jax
import jax.numpy as jnp
from jax import lax
from jax.experimental import pallas as pl
from jax.experimental.pallas import tpu as pltpu
from jax.sharding import PartitionSpec as P

MOST = 32
F32 = jnp.float32
BF16 = jnp.bfloat16
MIB = 1024 * 1024


def mm(left, right):
    return lax.dot_general(left, right, (((1,), (0,)), ((), ())), preferred_element_type=F32)


def mm_lead(left, right):
    return lax.dot_general(left, right, (((0,), (0,)), ((), ())), preferred_element_type=F32)


def mm_trail(left, right):
    return lax.dot_general(left, right, (((1,), (1,)), ((), ())), preferred_element_type=F32)


def params(mib):
    return pltpu.CompilerParams(vmem_limit_bytes=mib * MIB)


def hop(x, axis, offset):
    return lax.ppermute(x, axis, [(i, i ^ offset) for i in range(lax.axis_size(axis))])


def prep_kernel(pos, ids, gates, tokens, grads, *outs, n_f, n_e):
    sends, select = outs[:n_e], outs[n_e]
    f, e = pos[0], pos[1]
    tok = ids.shape[1]
    width = tokens.shape[1] // n_f
    rows = max(16, n_e)
    row = lax.broadcasted_iota(jnp.int32, (rows, tok), 0)
    chosen = []
    weight = []
    stacked = jnp.zeros((rows, tok), F32)
    for k in range(n_e):
        match = ids[...] == (e ^ k)
        chosen.append(jnp.max(jnp.where(match, 1.0, 0.0), axis=0, keepdims=True))
        weight.append(jnp.sum(jnp.where(match, gates[...].astype(F32), 0.0), axis=0, keepdims=True))
        stacked = jnp.where(row == k, chosen[k], stacked)
    before = lax.broadcasted_iota(jnp.int32, (tok, tok), 0) < lax.broadcasted_iota(jnp.int32, (tok, tok), 1)
    slot = mm(stacked.astype(BF16), jnp.where(before, 1.0, 0.0).astype(BF16))
    want = lax.broadcasted_iota(jnp.int32, (MOST, tok), 0).astype(F32)
    picks = []
    scaled = []
    for k in range(n_e):
        hit = jnp.where(want == slot[k : k + 1], chosen[k], 0.0)
        picks.append(hit)
        scaled.append(hit * weight[k])
    picks = jnp.concatenate(picks, axis=0).astype(BF16)
    scaled = jnp.concatenate(scaled, axis=0).astype(BF16)
    select[...] = picks
    for j in range(n_f):
        at = pl.ds(pl.multiple_of((f ^ j) * width, width), width)
        here = slice(j * width, (j + 1) * width)
        x = mm(picks, tokens[:, at]).astype(BF16)
        q = mm(scaled, grads[:, at]).astype(BF16)
        for k in range(n_e):
            sends[k][:MOST, here] = x[k * MOST : (k + 1) * MOST]
            sends[k][MOST:, here] = q[k * MOST : (k + 1) * MOST]


def pack_kernel(*refs, n_f, n_e):
    recv, outs = refs[:n_e], refs[n_e:]
    width = recv[0].shape[1] // n_f
    rows = n_e * MOST
    for c, out in enumerate(outs):
        for side in range(2):
            j = 2 * c + side
            here = slice(j * width, (j + 1) * width)
            for k in range(n_e):
                out[side, k * MOST : (k + 1) * MOST] = recv[k][:MOST, here]
                out[side, rows + k * MOST : rows + (k + 1) * MOST] = recv[k][MOST:, here]


def up_kernel(*refs, n_f, n_e):
    recv = refs[:n_e]
    gates, ups = refs[n_e : n_e + n_f], refs[n_e + n_f : n_e + 2 * n_f]
    a_out, b_out = refs[n_e + 2 * n_f :]
    width = recv[0].shape[1] // n_f
    a = b = None
    for j in range(n_f):
        here = slice(j * width, (j + 1) * width)
        x = jnp.concatenate([r[:MOST, here] for r in recv], axis=0)
        pa, pb = mm(x, gates[j][...]), mm(x, ups[j][...])
        a, b = (pa, pb) if a is None else (a + pa, b + pb)
    a_out[...] = a
    b_out[...] = b


def delta_kernel(*refs, n_f, n_e):
    recv = refs[:n_e]
    low, high = refs[n_e : n_e + n_f], refs[n_e + n_f : n_e + 2 * n_f]
    a_in, b_in, first, second, pick_out = refs[n_e + 2 * n_f :]
    width = recv[0].shape[1] // n_f
    hidden = a_in.shape[1]
    r = None
    for j in range(n_f):
        here = slice(j * width, (j + 1) * width)
        q = jnp.concatenate([rows[MOST:, here] for rows in recv], axis=0)
        part = mm(q, jnp.concatenate([low[j][...], high[j][...]], axis=0))
        r = part if r is None else r + part
    a, b = a_in[...], b_in[...]
    s = jax.nn.sigmoid(a)
    silu = a * s
    h = (silu * b).astype(BF16)
    pick = jnp.sum(h.astype(F32) * r, axis=1, keepdims=True)
    da = (r * b * s * (1.0 + a * (1.0 - s))).astype(BF16)
    du = (r * silu).astype(BF16)
    half = a.shape[0] // 2
    for out, rows in ((first, slice(0, half)), (second, slice(half, 2 * half))):
        out[:, :hidden] = da[rows]
        out[:, hidden : 2 * hidden] = du[rows]
        out[:, 2 * hidden :] = h[rows]
    coarse = pick.astype(BF16)
    fine = (pick - coarse.astype(F32)).astype(BF16)
    lane = lax.broadcasted_iota(jnp.int32, pick_out.shape, 1)
    wide = pick_out.shape
    pick_out[...] = jnp.where(
        lane < wide[1] // 2, jnp.broadcast_to(coarse.astype(F32), wide), jnp.broadcast_to(fine.astype(F32), wide)
    ).astype(BF16)


def back_kernel(*refs, n_f, n_e):
    first, second, pick = refs[:3]
    gates, ups = refs[3 : 3 + n_f], refs[3 + n_f : 3 + 2 * n_f]
    outs = refs[3 + 2 * n_f :]
    width, hidden = gates[0].shape
    da = jnp.concatenate([first[:, :hidden], second[:, :hidden]], axis=0)
    du = jnp.concatenate([first[:, hidden : 2 * hidden], second[:, hidden : 2 * hidden]], axis=0)
    for j in range(n_f):
        c = (mm_trail(da, gates[j][...]) + mm_trail(du, ups[j][...])).astype(BF16)
        for k in range(n_e):
            outs[k][:, j * width : (j + 1) * width] = c[k * MOST : (k + 1) * MOST]
    for k in range(n_e):
        outs[k][:, n_f * width :] = pick[k * MOST : (k + 1) * MOST]


def weight_kernel(*refs, n_f):
    rows_of, firsts, seconds = refs[:n_f], refs[n_f : 2 * n_f], refs[2 * n_f : 3 * n_f]
    grad_gate, grad_up, grad_down = refs[3 * n_f :]
    hidden = grad_gate.shape[1]
    count = 2 * firsts[0].shape[0]
    both = down = None
    for j in range(n_f):
        side = j % 2
        x, q = rows_of[j][side, :count], rows_of[j][side, count:]
        d = jnp.concatenate([firsts[j][...], seconds[j][...]], axis=0)
        pb, pd = mm_lead(x, d[:, : 2 * hidden]), mm_lead(q, d[:, 2 * hidden :])
        both, down = (pb, pd) if both is None else (both + pb, down + pd)
    grad_gate[...] = both[:, :hidden].astype(BF16)
    grad_up[...] = both[:, hidden:].astype(BF16)
    grad_down[...] = down.astype(BF16)


def final_kernel(pos, ids, gates, select, *refs, n_f, n_e):
    back, in_grad, gate_grad = refs[:n_e], refs[n_e], refs[n_e + 1]
    f, e = pos[0], pos[1]
    width = in_grad.shape[1] // n_f
    total = n_f * width
    for j in range(n_f):
        at = pl.ds(pl.multiple_of((f ^ j) * width, width), width)
        c = jnp.concatenate([b[:, j * width : (j + 1) * width] for b in back], axis=0)
        in_grad[:, at] = mm_lead(select[...], c).astype(BF16)
    half = (back[0].shape[1] - total) // 2
    found = jnp.zeros(ids.shape, F32)
    for k in range(n_e):
        pick = back[k][:, total : total + 1].astype(F32) + back[k][:, total + half : total + half + 1].astype(F32)
        hit = select[k * MOST : (k + 1) * MOST].astype(F32)
        value = jnp.sum(hit * pick, axis=0, keepdims=True)
        found = found + jnp.where(ids[...] == (e ^ k), value, 0.0)
    gate_grad[...] = (found / gates[...].astype(F32)).astype(BF16)


def call(kernel, outs, mib, **static):
    return pl.pallas_call(functools.partial(kernel, **static), out_shape=outs, compiler_params=params(mib))


def call_at(kernel, inputs, outs, mib, **static):
    return pl.pallas_call(
        functools.partial(kernel, **static),
        out_shape=outs,
        in_specs=[pl.BlockSpec(memory_space=pltpu.SMEM)] + [pl.BlockSpec(memory_space=pltpu.VMEM)] * (inputs - 1),
        compiler_params=params(mib),
    )


def spread(x, bits):
    have = {0: x}
    for bit in bits:
        have.update({o ^ bit: hop(v, "fsdp", bit) for o, v in list(have.items())})
    return have


def swap_cores(have):
    return have | {o ^ 1: hop(v, "fsdp", 1) for o, v in have.items()}


def in_order(have):
    return [have[j] for j in range(len(have))]


def per_device(tokens, out_grad, expert_ids, gate_probs, w_gate, w_up, w_down):
    tok, model = tokens.shape
    local, _, hidden = w_gate.shape
    n_f, n_e = lax.axis_size("fsdp"), lax.axis_size("ep")
    rows = n_e * MOST
    sizes = dict(n_f=n_f, n_e=n_e)
    bits = [1 << i for i in range(1, n_f.bit_length() - 1)]
    mirrored = bits[::-1]
    shape = jax.ShapeDtypeStruct

    down = w_down[:, 0]
    gate_at = spread(w_gate[:, 0], bits)
    up_at = spread(w_up[:, 0], mirrored)
    low_at = spread(down[: local // 2], bits)
    high_at = spread(down[local // 2 :], mirrored)
    gate_at, up_at, low_at, high_at = map(in_order, map(swap_cores, (gate_at, up_at, low_at, high_at)))

    pos = jnp.stack([lax.axis_index("fsdp"), lax.axis_index("ep")]).astype(jnp.int32)
    ids, gates = expert_ids.T, gate_probs.T
    *sends, select = call_at(
        prep_kernel, 5, [shape((2 * MOST, model), BF16)] * n_e + [shape((rows, tok), BF16)], 16, **sizes
    )(pos, ids, gates, tokens, out_grad)
    recv = [sends[0]] + [hop(sends[k], "ep", k) for k in range(1, n_e)]

    packed = call(pack_kernel, [shape((2, 2 * rows, local), BF16)] * (n_f // 2), 8, **sizes)(*recv)
    rows_at = {0: packed[0]} | {2 * c: hop(packed[c], "fsdp", 2 * c) for c in range(1, n_f // 2)}
    rows_at = in_order(swap_cores(rows_at))

    a, b = call(up_kernel, [shape((rows, hidden), F32)] * 2, 16, **sizes)(*recv, *gate_at, *up_at)
    first, second, pick = call(
        delta_kernel, [shape((rows // 2, 3 * hidden), BF16)] * 2 + [shape((rows, 128), BF16)], 16, **sizes
    )(*recv, *low_at, *high_at, a, b)

    first_at = in_order(swap_cores(spread(first, bits)))
    second_at = in_order(swap_cores(spread(second, mirrored)))

    back = call(back_kernel, [shape((MOST, model + 128), BF16)] * n_e, 16, **sizes)(
        first, second, pick, *gate_at, *up_at
    )
    back = [back[0]] + [hop(back[k], "ep", k) for k in range(1, n_e)]
    in_grad, gate_grad = call_at(
        final_kernel, 4 + n_e, [shape((tok, model), BF16), shape(ids.shape, BF16)], 16, **sizes
    )(pos, ids, gates, select, *back)

    grads = call(weight_kernel, [shape((local, hidden), BF16)] * 3, 24, n_f=n_f)(*rows_at, *first_at, *second_at)
    return (in_grad, gate_grad.T, *(g[:, None] for g in grads))


def solution(mesh):
    tok = P(("fsdp", "ep"), None)
    weight = P("fsdp", "ep", None)
    return jax.shard_map(
        per_device,
        mesh=mesh,
        in_specs=(tok, tok, tok, tok, weight, weight, weight),
        out_specs=(tok, tok, weight, weight, weight),
        check_vma=False,
    )
```

```python
import functools

import jax
import jax.numpy as jnp
from jax import lax
from jax.experimental import pallas as pl
from jax.experimental.pallas import tpu as pltpu
from jax.sharding import PartitionSpec as P

MOST = 32
F32 = jnp.float32
BF16 = jnp.bfloat16
MIB = 1024 * 1024


def mm(left, right):
    return lax.dot_general(left, right, (((1,), (0,)), ((), ())), preferred_element_type=F32)


def mm_lead(left, right):
    return lax.dot_general(left, right, (((0,), (0,)), ((), ())), preferred_element_type=F32)


def mm_trail(left, right):
    return lax.dot_general(left, right, (((1,), (1,)), ((), ())), preferred_element_type=F32)


def hop(x, axis, offset):
    return lax.ppermute(x, axis, [(i, i ^ offset) for i in range(lax.axis_size(axis))])


class Copies:
    def __init__(self, sems):
        self.sems, self.made, self.waited = sems, [], 0

    def start(self, source, target):
        self.made.append(pltpu.make_async_copy(source, target, self.sems.at[len(self.made)]))
        self.made[-1].start()

    def wait(self, count=None):
        for copy in self.made[self.waited : None if count is None else self.waited + count]:
            copy.wait()
            self.waited += 1


def split_kernel(gate, up, down, first, second, sems):
    width = gate.shape[0]
    half = width // 2
    fetch = Copies(sems)
    fetch.start(gate, first.at[:width])
    fetch.start(down.at[:half], first.at[width:])
    fetch.start(up, second.at[:width])
    fetch.start(down.at[half:], second.at[width:])
    fetch.wait()


def prep_kernel(pos, ids, gates, tokens_in, grads_in, *refs, n_f, n_e):
    sends, select = refs[:n_e], refs[n_e]
    tokens, grads, sems = refs[n_e + 1 :]
    fetch = [
        pltpu.make_async_copy(tokens_in, tokens, sems.at[0]),
        pltpu.make_async_copy(grads_in, grads, sems.at[1]),
    ]
    for copy in fetch:
        copy.start()
    f, e = pos[0], pos[1]
    tok = ids.shape[1]
    width = tokens.shape[1] // n_f
    rows = max(16, n_e)
    row = lax.broadcasted_iota(jnp.int32, (rows, tok), 0)
    chosen = []
    weight = []
    stacked = jnp.zeros((rows, tok), F32)
    for k in range(n_e):
        match = ids[...] == (e ^ k)
        chosen.append(jnp.max(jnp.where(match, 1.0, 0.0), axis=0, keepdims=True))
        weight.append(jnp.sum(jnp.where(match, gates[...].astype(F32), 0.0), axis=0, keepdims=True))
        stacked = jnp.where(row == k, chosen[k], stacked)
    before = lax.broadcasted_iota(jnp.int32, (tok, tok), 0) < lax.broadcasted_iota(jnp.int32, (tok, tok), 1)
    slot = mm(stacked.astype(BF16), jnp.where(before, 1.0, 0.0).astype(BF16))
    want = lax.broadcasted_iota(jnp.int32, (MOST, tok), 0).astype(F32)
    picks = []
    scaled = []
    for k in range(n_e):
        hit = jnp.where(want == slot[k : k + 1], chosen[k], 0.0)
        picks.append(hit)
        scaled.append(hit * weight[k])
    picks = jnp.concatenate(picks, axis=0).astype(BF16)
    scaled = jnp.concatenate(scaled, axis=0).astype(BF16)
    select[...] = picks
    for copy in fetch:
        copy.wait()
    for j in range(n_f):
        at = pl.ds(pl.multiple_of((f ^ j) * width, width), width)
        here = slice(j // 2 * width, (j // 2 + 1) * width)
        x = mm(picks, tokens[:, at]).astype(BF16)
        q = mm(scaled, grads[:, at]).astype(BF16)
        for k in range(n_e):
            sends[k][j % 2, :MOST, here] = x[k * MOST : (k + 1) * MOST]
            sends[k][j % 2, MOST:, here] = q[k * MOST : (k + 1) * MOST]


def pack_kernel(*refs, n_e):
    sides = refs[:n_e], refs[n_e : 2 * n_e]
    outs = refs[2 * n_e :]
    width = outs[0].shape[2]
    rows = n_e * MOST
    for i, out in enumerate(outs):
        here = slice((i + 1) * width, (i + 2) * width)
        for side in range(2):
            for k in range(n_e):
                out[side, k * MOST : (k + 1) * MOST] = sides[side][k][side, :MOST, here]
                out[side, rows + k * MOST : rows + (k + 1) * MOST] = sides[side][k][side, MOST:, here]


def forward_kernel(*refs, n_e, entries, carried):
    sides = refs[:n_e], refs[n_e : 2 * n_e]
    refs = refs[2 * n_e :]
    if carried:
        total_in, refs = refs[0], refs[1:]
    count = len(entries)
    firsts, seconds, refs = refs[:count], refs[count : 2 * count], refs[2 * count :]
    outs, (gate, up, down, sems) = refs[:-4], refs[-4:]
    hidden = gate.shape[1]
    width = gate.shape[0] // count
    half = width // 2
    fetch = Copies(sems)
    for i in range(count):
        fetch.start(firsts[i].at[:width], gate.at[pl.ds(i * width, width)])
        fetch.start(seconds[i].at[:width], up.at[pl.ds(i * width, width)])
        fetch.start(firsts[i].at[width:], down.at[pl.ds(i * width, half)])
        fetch.start(seconds[i].at[width:], down.at[pl.ds(i * width + half, half)])

    def rows_of(part):
        return jnp.concatenate(
            [
                jnp.concatenate([sides[side][k][side, part, i * width : (i + 1) * width] for i in entries], axis=1)
                for side in range(2)
                for k in range(n_e)
            ],
            axis=0,
        )

    x, q = rows_of(slice(0, MOST)), rows_of(slice(MOST, 2 * MOST))
    fetch.wait()
    rows = n_e * MOST
    for at, (left, right) in enumerate(((x, gate), (x, up), (q, down))):
        here = slice(at * hidden, (at + 1) * hidden)
        part = mm(left, right[...])
        if carried:
            part = part + total_in[:, here]
            outs[0][:, here] = part[:rows]
            outs[1][:, here] = part[rows:].astype(BF16)
        else:
            outs[0][:, here] = part


def delta_kernel(own, got, first, second, pick_out):
    hidden = own.shape[1] // 3
    a, b, r = (
        own[:, at * hidden : (at + 1) * hidden] + got[:, at * hidden : (at + 1) * hidden].astype(F32) for at in range(3)
    )
    s = jax.nn.sigmoid(a)
    silu = a * s
    h = (silu * b).astype(BF16)
    pick = jnp.sum(h.astype(F32) * r, axis=1, keepdims=True)
    da = (r * b * s * (1.0 + a * (1.0 - s))).astype(BF16)
    du = (r * silu).astype(BF16)
    half = a.shape[0] // 2
    for out, rows in ((first, slice(0, half)), (second, slice(half, 2 * half))):
        out[:, :hidden] = da[rows]
        out[:, hidden : 2 * hidden] = du[rows]
        out[:, 2 * hidden :] = h[rows]
    coarse = pick.astype(BF16)
    fine = (pick - coarse.astype(F32)).astype(BF16)
    wide = pick_out.shape
    lane = lax.broadcasted_iota(jnp.int32, wide, 1)
    pick_out[...] = jnp.where(
        lane < wide[1] // 2, jnp.broadcast_to(coarse.astype(F32), wide), jnp.broadcast_to(fine.astype(F32), wide)
    ).astype(BF16)


def back_kernel(first, second, first_other, second_other, pick, *refs, n, n_e):
    firsts, seconds, outs = refs[:n], refs[n : 2 * n], refs[2 * n : 2 * n + n_e]
    gate, up, sems = refs[2 * n + n_e :]
    hidden = gate.shape[2]
    width = gate.shape[1]
    fetch = Copies(sems)
    for i in range(n):
        fetch.start(firsts[i].at[:width], gate.at[i])
        fetch.start(seconds[i].at[:width], up.at[i])
    parts = (first, second, first_other, second_other)
    da = jnp.concatenate([p[:, :hidden] for p in parts], axis=0)
    du = jnp.concatenate([p[:, hidden : 2 * hidden] for p in parts], axis=0)
    for i in range(n):
        fetch.wait(2)
        c = (mm_trail(da, gate[i]) + mm_trail(du, up[i])).astype(BF16)
        here = slice(i * width, (i + 1) * width)
        for side in range(2):
            for k in range(n_e):
                at = (side * n_e + k) * MOST
                outs[k][side, :, here] = c[at : at + MOST]
    for side in range(2):
        for k in range(n_e):
            outs[k][side, :, n * width :] = pick[k * MOST : (k + 1) * MOST]


def weight_kernel(*refs, n_e, entries, carried):
    if 0 in entries:
        sides, refs = (refs[:n_e], refs[n_e : 2 * n_e]), refs[2 * n_e :]
    if carried:
        total_in, refs = refs[0], refs[1:]
    far = [i for i in entries if i]
    got, deltas = refs[: len(far)], refs[len(far) : len(far) + 4 * len(entries)]
    outs, (x, q, d, sems) = refs[len(far) + 4 * len(entries) : -4], refs[-4:]
    width, hidden = x.shape[1], d.shape[1] // 3
    rows = n_e * MOST
    fetch = Copies(sems)
    for i, p in enumerate(deltas):
        fetch.start(p, d.at[pl.ds(i * rows // 2, rows // 2)])
    for place, i in enumerate(entries):
        if i == 0:
            continue
        for side in range(2):
            at = pl.ds((2 * place + side) * rows, rows)
            fetch.start(got[far.index(i)].at[side, :rows], x.at[at])
            fetch.start(got[far.index(i)].at[side, rows:], q.at[at])
    if 0 in entries:
        for side in range(2):
            for k in range(n_e):
                at = slice(side * rows + k * MOST, side * rows + (k + 1) * MOST)
                x[at] = sides[side][k][side, :MOST, :width]
                q[at] = sides[side][k][side, MOST:, :width]
    fetch.wait()
    for at, left in enumerate((x, x, q)):
        here = slice(at * hidden, (at + 1) * hidden)
        part = mm_lead(left[...], d[:, here])
        if carried:
            outs[at][...] = (total_in[:, here] + part).astype(BF16)
        else:
            outs[0][:, here] = part


def final_kernel(pos, ids, gates, select, *refs, n_f, n_e):
    mine, other, (in_grad, gate_grad) = refs[:n_e], refs[n_e : 2 * n_e], refs[2 * n_e :]
    f, e = pos[0], pos[1]
    width = in_grad.shape[1] // n_f
    total = n_f // 2 * width
    for j in range(n_f):
        at = pl.ds(pl.multiple_of((f ^ j) * width, width), width)
        here = slice(j // 2 * width, (j // 2 + 1) * width)
        c = jnp.concatenate([(other if j % 2 else mine)[k][j % 2, :, here] for k in range(n_e)], axis=0)
        in_grad[:, at] = mm_lead(select[...], c).astype(BF16)
    half = (mine[0].shape[2] - total) // 2
    found = jnp.zeros(ids.shape, F32)
    for k in range(n_e):
        pick = mine[k][0, :, total : total + 1].astype(F32) + mine[k][0, :, total + half : total + half + 1].astype(F32)
        hit = select[k * MOST : (k + 1) * MOST].astype(F32)
        value = jnp.sum(hit * pick, axis=0, keepdims=True)
        found = found + jnp.where(ids[...] == (e ^ k), value, 0.0)
    gate_grad[...] = (found / gates[...].astype(F32)).astype(BF16)


def call(kernel, args, places, outs, mib, scratch=(), places_out=None, **static):
    spaces = {"s": pltpu.SMEM, "v": pltpu.VMEM, "a": pl.ANY}
    return pl.pallas_call(
        functools.partial(kernel, **static),
        out_shape=outs,
        in_specs=[pl.BlockSpec(memory_space=spaces[p]) for p in places],
        **({"out_specs": [pl.BlockSpec(memory_space=spaces[p]) for p in places_out]} if places_out else {}),
        scratch_shapes=scratch,
        compiler_params=pltpu.CompilerParams(vmem_limit_bytes=mib * MIB),
    )(*args)


def low_bit(o):
    return o & -o


def high_bit(o):
    return 1 << (o.bit_length() - 1)


def after(x, *needs):
    return lax.optimization_barrier((x, *needs))[0] if needs else x


def to_neighbours(first, second, bits):
    first_at, second_at = {0: first}, {0: second}
    for bit in bits:
        if bit == bits[0]:
            first_at[bit] = hop(first, "fsdp", bit)
        else:
            second_at[bit] = hop(second, "fsdp", bit)
    for bit in bits:
        if bit == bits[0]:
            second_at[bit] = hop(second, "fsdp", bit)
        else:
            first_at[bit] = hop(first, "fsdp", bit)
    return first_at, second_at


def to_others(first_at, second_at, routed, waits):
    for o in routed:
        first_at[o] = hop(after(first_at[o ^ high_bit(o)], *waits[0]), "fsdp", high_bit(o))
        second_at[o] = hop(after(second_at[o ^ low_bit(o)], *waits[1]), "fsdp", low_bit(o))


def per_device(tokens, out_grad, expert_ids, gate_probs, w_gate, w_up, w_down):
    tok, model = tokens.shape
    local, _, hidden = w_gate.shape
    n_f, n_e = lax.axis_size("fsdp"), lax.axis_size("ep")
    rows = n_e * MOST
    n = n_f // 2
    bits = [1 << i for i in range(1, n_f.bit_length() - 1)]
    routed = [o for o in range(2, n_f, 2) if o != low_bit(o)]
    shape = jax.ShapeDtypeStruct

    piece = shape((local + local // 2, hidden), BF16)
    pieces = call(
        split_kernel, (w_gate[:, 0], w_up[:, 0], w_down[:, 0]), "aaa", [piece] * 2, 8, [pltpu.SemaphoreType.DMA((4,))], places_out="aa"
    )
    weights = to_neighbours(*pieces, bits)

    pos = jnp.stack([lax.axis_index("fsdp"), lax.axis_index("ep")]).astype(jnp.int32)
    ids, gates = expert_ids.T, gate_probs.T
    *sends, select = call(
        prep_kernel,
        (pos, ids, gates, tokens, out_grad),
        "svvaa",
        [shape((2, 2 * MOST, model // 2), BF16)] * n_e + [shape((rows, tok), BF16)],
        16,
        [pltpu.VMEM(tokens.shape, BF16)] * 2 + [pltpu.SemaphoreType.DMA((2,))],
        n_f=n_f,
        n_e=n_e,
    )
    mine = [sends[0]] + [None] * (n_e - 1)
    early = [(), (weights[0][bits[0]],), (weights[1][bits[-1]],)]
    for turn, k in enumerate(range(n_e - 1, 0, -1)):
        mine[k] = hop(after(sends[k], *(early[turn] if turn < 3 else (mine[k + 3],))), "ep", k)
    to_others(*weights, routed, ((mine[-1],), (mine[1],)))
    weights = [[w[o] for o in range(0, n_f, 2)] for w in weights]
    other = [hop(m, "fsdp", 1) for m in mine]
    both = (*mine, *other)

    packed = call(
        pack_kernel, both, "v" * 2 * n_e, [shape((2, 2 * rows, local), BF16)] * (n - 1), 16, n_e=n_e
    )
    got = [hop(p, "fsdp", 2 * i + 2) for i, p in enumerate(packed)]

    def forward(entries, carried):
        pieces = [w[i] for w in weights for i in entries]
        size = len(entries) * local
        return call(
            forward_kernel,
            (*both, *carried, *pieces),
            "v" * (2 * n_e + len(carried)) + "a" * len(pieces),
            [shape((rows, 3 * hidden), F32), shape((rows, 3 * hidden), BF16)]
            if carried
            else [shape((2 * rows, 3 * hidden), F32)],
            24,
            [pltpu.VMEM((size, hidden), BF16)] * 3 + [pltpu.SemaphoreType.DMA((4 * len(entries),))],
            n_e=n_e,
            entries=entries,
            carried=bool(carried),
        )

    late = [o // 2 for o in routed]
    own, theirs = forward(late, forward([i for i in range(n) if i not in late], ()))
    first, second, pick = call(
        delta_kernel,
        (own, hop(theirs, "fsdp", 1)),
        "vv",
        [shape((rows // 2, 3 * hidden), BF16)] * 2 + [shape((rows, 128), BF16)],
        16,
    )

    firsts, seconds = to_neighbours(first, second, bits)
    first_other, second_other = hop(first, "fsdp", 1), hop(second, "fsdp", 1)

    backs = call(
        back_kernel,
        (first, second, first_other, second_other, pick, *weights[0], *weights[1]),
        "vvvvv" + "a" * 2 * n,
        [shape((2, MOST, model // 2 + 128), BF16)] * n_e,
        16,
        [pltpu.VMEM((n, local, hidden), BF16)] * 2 + [pltpu.SemaphoreType.DMA((2 * n,))],
        n=n,
        n_e=n_e,
    )
    back = [backs[0]] + [None] * (n_e - 1)
    early = [(), (firsts[bits[0]],), (seconds[bits[-1]],)]
    for turn, k in enumerate(range(n_e - 1, 0, -1)):
        back[k] = hop(after(backs[k], *(early[turn] if turn < 3 else (back[k + 3],))), "ep", k)
    to_others(firsts, seconds, routed, ((back[-1],), (back[1],)))
    backs = (*back, *(hop(b, "fsdp", 1) for b in back))
    in_grad, gate_grad = call(
        final_kernel,
        (pos, ids, gates, select, *backs),
        "svvv" + "v" * 2 * n_e,
        [shape((tok, model), BF16), shape(ids.shape, BF16)],
        16,
        n_f=n_f,
        n_e=n_e,
    )

    firsts_other, seconds_other = {0: first_other}, {0: second_other}
    for o in bits + routed:
        firsts_other[o], seconds_other[o] = hop(firsts[o], "fsdp", 1), hop(seconds[o], "fsdp", 1)

    def weight_sums(entries, carried):
        far = [got[i - 1] for i in entries if i]
        deltas = [at[2 * i] for i in entries for at in (firsts, seconds, firsts_other, seconds_other)]
        size = 2 * rows * len(entries)
        near = both if 0 in entries else ()
        return call(
            weight_kernel,
            (*near, *carried, *far, *deltas),
            "v" * (len(near) + len(carried)) + "a" * (len(far) + len(deltas)),
            [shape((local, hidden), BF16)] * 3 if carried else [shape((local, 3 * hidden), F32)],
            24,
            [pltpu.VMEM((size, local), BF16)] * 2
            + [pltpu.VMEM((size, 3 * hidden), BF16), pltpu.SemaphoreType.DMA((4 * len(far) + len(deltas),))],
            n_e=n_e,
            entries=entries,
            carried=bool(carried),
        )

    grads = weight_sums(late, weight_sums([i for i in range(n) if i not in late], ()))
    return (in_grad, gate_grad.T, *(g[:, None] for g in grads))


def solution(mesh):
    tok = P(("fsdp", "ep"), None)
    weight = P("fsdp", "ep", None)
    return jax.shard_map(
        per_device,
        mesh=mesh,
        in_specs=(tok, tok, tok, tok, weight, weight, weight),
        out_specs=(tok, tok, weight, weight, weight),
        check_vma=False,
    )
```

```python
import functools
import itertools

import jax
import jax.numpy as jnp
from jax import lax
from jax.experimental import pallas as pl
from jax.experimental.pallas import tpu as pltpu
from jax.sharding import PartitionSpec as P

MOST = 32
F32 = jnp.float32
BF16 = jnp.bfloat16
MIB = 1024 * 1024
HINT = pl.CostEstimate(flops=5_000_000_000, bytes_accessed=15_000_000, transcendentals=0)


def mm(left, right):
    return lax.dot_general(left, right, (((1,), (0,)), ((), ())), preferred_element_type=F32)


def mm_lead(left, right):
    return lax.dot_general(left, right, (((0,), (0,)), ((), ())), preferred_element_type=F32)


def mm_trail(left, right):
    return lax.dot_general(left, right, (((1,), (1,)), ((), ())), preferred_element_type=F32)


def hop(x, axis, offset):
    return lax.ppermute(x, axis, [(i, i ^ offset) for i in range(lax.axis_size(axis))])


def flips(position, core, bits):
    return sum(2 << (bits - 1 - b if core else b) for b in range(bits) if position >> b & 1)


def mirror(position, bits):
    return flips(position, 1, bits) // 2


def slice_of(f, side, position, n_f):
    bits = n_f.bit_length() - 2
    even, odd = flips(position, 0, bits), flips(position, 1, bits)
    return f ^ side ^ (even + ((f ^ side) & 1) * (odd - even))


class Copies:
    def __init__(self, sems):
        self.sems, self.made, self.waited = sems, [], 0

    def start(self, source, target):
        self.made.append(pltpu.make_async_copy(source, target, self.sems.at[len(self.made)]))
        self.made[-1].start()

    def wait(self, count=None):
        for copy in self.made[self.waited : None if count is None else self.waited + count]:
            copy.wait()
            self.waited += 1


def stack_kernel(*refs):
    parts, (out, sems) = refs[:-2], refs[-2:]
    fetch = Copies(sems)
    size = parts[0].shape[0]
    for i, part in enumerate(parts):
        fetch.start(part, out.at[pl.ds(i * size, size)])
    fetch.wait()


def prep_kernel(pos, ids, gates, tokens_in, grads_in, *refs, n_f, n_e):
    sends, select = refs[:n_e], refs[n_e]
    tokens, grads, sems = refs[n_e + 1 :]
    fetch = [
        pltpu.make_async_copy(tokens_in, tokens, sems.at[0]),
        pltpu.make_async_copy(grads_in, grads, sems.at[1]),
    ]
    for copy in fetch:
        copy.start()
    f, e = pos[0], pos[1]
    tok = ids.shape[1]
    width = tokens.shape[1] // n_f
    rows = max(16, n_e)
    row = lax.broadcasted_iota(jnp.int32, (rows, tok), 0)
    chosen = []
    weight = []
    stacked = jnp.zeros((rows, tok), F32)
    for k in range(n_e):
        match = ids[...] == (e ^ k)
        chosen.append(jnp.max(jnp.where(match, 1.0, 0.0), axis=0, keepdims=True))
        weight.append(jnp.sum(jnp.where(match, gates[...].astype(F32), 0.0), axis=0, keepdims=True))
        stacked = jnp.where(row == k, chosen[k], stacked)
    before = lax.broadcasted_iota(jnp.int32, (tok, tok), 0) < lax.broadcasted_iota(jnp.int32, (tok, tok), 1)
    slot = mm(stacked.astype(BF16), jnp.where(before, 1.0, 0.0).astype(BF16))
    want = lax.broadcasted_iota(jnp.int32, (MOST, tok), 0).astype(F32)
    picks = []
    scaled = []
    for k in range(n_e):
        hit = jnp.where(want == slot[k : k + 1], chosen[k], 0.0)
        picks.append(hit)
        scaled.append(hit * weight[k])
    picks = jnp.concatenate(picks, axis=0).astype(BF16)
    scaled = jnp.concatenate(scaled, axis=0).astype(BF16)
    select[...] = picks
    for copy in fetch:
        copy.wait()
    for side, position in itertools.product(range(2), range(n_f // 2)):
        at = pl.ds(pl.multiple_of(slice_of(f, side, position, n_f) * width, width), width)
        here = slice(position * width, (position + 1) * width)
        x = mm(picks, tokens[:, at]).astype(BF16)
        q = mm(scaled, grads[:, at]).astype(BF16)
        for k in range(n_e):
            sends[k][side, :MOST, here] = x[k * MOST : (k + 1) * MOST]
            sends[k][side, MOST:, here] = q[k * MOST : (k + 1) * MOST]


def pack_kernel(*refs, n_e):
    sides = refs[:n_e], refs[n_e : 2 * n_e]
    outs = refs[2 * n_e :]
    width = outs[0].shape[2]
    rows = n_e * MOST
    for i, out in enumerate(outs):
        here = slice((i + 1) * width, (i + 2) * width)
        for side in range(2):
            for k in range(n_e):
                out[side, k * MOST : (k + 1) * MOST] = sides[side][k][side, :MOST, here]
                out[side, rows + k * MOST : rows + (k + 1) * MOST] = sides[side][k][side, MOST:, here]


def forward_kernel(*refs, n_e, entries, carried):
    sides = refs[:n_e], refs[n_e : 2 * n_e]
    refs = refs[2 * n_e :]
    if carried:
        total_in, refs = refs[0], refs[1:]
    count = len(entries)
    pieces, refs = refs[:count], refs[count:]
    outs, (gate, up, down, sems) = refs[:-4], refs[-4:]
    hidden = gate.shape[1]
    width = gate.shape[0] // count
    fetch = Copies(sems)
    for at, whole in enumerate((gate, up, down)):
        for i in range(count):
            fetch.start(pieces[i].at[pl.ds(at * width, width)], whole.at[pl.ds(i * width, width)])

    def rows_of(part):
        return jnp.concatenate(
            [
                jnp.concatenate([sides[side][k][side, part, i * width : (i + 1) * width] for i in entries], axis=1)
                for side in range(2)
                for k in range(n_e)
            ],
            axis=0,
        )

    x, q = rows_of(slice(0, MOST)), rows_of(slice(MOST, 2 * MOST))
    rows = n_e * MOST
    for at, (left, right) in enumerate(((x, gate), (x, up), (q, down))):
        fetch.wait(count)
        here = slice(at * hidden, (at + 1) * hidden)
        part = mm(left, right[...])
        if carried:
            part = part + total_in[:, here]
            outs[0][:, here] = part[:rows]
            outs[1][:, here] = part[rows:].astype(BF16)
        else:
            outs[0][:, here] = part


def delta_kernel(own, got, deltas, pick_out):
    hidden = own.shape[1] // 3
    a, b, r = (
        own[:, at * hidden : (at + 1) * hidden] + got[:, at * hidden : (at + 1) * hidden].astype(F32) for at in range(3)
    )
    s = jax.nn.sigmoid(a)
    silu = a * s
    h = (silu * b).astype(BF16)
    pick = jnp.sum(h.astype(F32) * r, axis=1, keepdims=True)
    deltas[:, :hidden] = (r * b * s * (1.0 + a * (1.0 - s))).astype(BF16)
    deltas[:, hidden : 2 * hidden] = (r * silu).astype(BF16)
    deltas[:, 2 * hidden :] = h
    coarse = pick.astype(BF16)
    fine = (pick - coarse.astype(F32)).astype(BF16)
    wide = pick_out.shape
    lane = lax.broadcasted_iota(jnp.int32, wide, 1)
    pick_out[...] = jnp.where(
        lane < wide[1] // 2, jnp.broadcast_to(coarse.astype(F32), wide), jnp.broadcast_to(fine.astype(F32), wide)
    ).astype(BF16)


def back_kernel(deltas, deltas_other, pick, *refs, n, n_e):
    pieces, outs, (gate, up, sems) = refs[:n], refs[n : n + n_e], refs[n + n_e :]
    hidden = gate.shape[2]
    width = gate.shape[1]
    fetch = Copies(sems)
    for i in range(n):
        fetch.start(pieces[i].at[:width], gate.at[i])
        fetch.start(pieces[i].at[pl.ds(width, width)], up.at[i])
    da = jnp.concatenate([deltas[:, :hidden], deltas_other[:, :hidden]], axis=0)
    du = jnp.concatenate([deltas[:, hidden : 2 * hidden], deltas_other[:, hidden : 2 * hidden]], axis=0)
    for i in range(n):
        fetch.wait(2)
        c = (mm_trail(da, gate[i]) + mm_trail(du, up[i])).astype(BF16)
        here = slice(i * width, (i + 1) * width)
        for side in range(2):
            for k in range(n_e):
                at = (side * n_e + k) * MOST
                outs[k][side, :, here] = c[at : at + MOST]
    for side in range(2):
        for k in range(n_e):
            outs[k][side, :, n * width :] = pick[k * MOST : (k + 1) * MOST]


def weight_kernel(*refs, n_e, entries, carried):
    if 0 in entries:
        sides, refs = (refs[:n_e], refs[n_e : 2 * n_e]), refs[2 * n_e :]
    if carried:
        total_in, refs = refs[0], refs[1:]
    far = [i for i in entries if i]
    got, deltas = refs[: len(far)], refs[len(far) : len(far) + 2 * len(entries)]
    outs, (x, q, d, sems) = refs[len(far) + 2 * len(entries) : -4], refs[-4:]
    width, hidden = x.shape[1], d.shape[1] // 3
    rows = n_e * MOST
    fetch = Copies(sems)
    for i, p in enumerate(deltas):
        fetch.start(p, d.at[pl.ds(i * rows, rows)])
    for place, i in enumerate(entries):
        if i == 0:
            continue
        for side in range(2):
            at = pl.ds((2 * place + side) * rows, rows)
            fetch.start(got[far.index(i)].at[side, :rows], x.at[at])
            fetch.start(got[far.index(i)].at[side, rows:], q.at[at])
    if 0 in entries:
        for side in range(2):
            for k in range(n_e):
                at = slice(side * rows + k * MOST, side * rows + (k + 1) * MOST)
                x[at] = sides[side][k][side, :MOST, :width]
                q[at] = sides[side][k][side, MOST:, :width]
    fetch.wait()
    for at, left in enumerate((x, x, q)):
        here = slice(at * hidden, (at + 1) * hidden)
        part = mm_lead(left[...], d[:, here])
        if carried:
            outs[at][...] = (total_in[:, here] + part).astype(BF16)
        else:
            outs[0][:, here] = part


def final_kernel(pos, ids, gates, select, *refs, n_f, n_e):
    mine, other, (in_grad, gate_grad) = refs[:n_e], refs[n_e : 2 * n_e], refs[2 * n_e :]
    f, e = pos[0], pos[1]
    width = in_grad.shape[1] // n_f
    total = n_f // 2 * width
    for side, position in itertools.product(range(2), range(n_f // 2)):
        at = pl.ds(pl.multiple_of(slice_of(f, side, position, n_f) * width, width), width)
        here = slice(position * width, (position + 1) * width)
        c = jnp.concatenate([(mine, other)[side][k][side, :, here] for k in range(n_e)], axis=0)
        in_grad[:, at] = mm_lead(select[...], c).astype(BF16)
    half = (mine[0].shape[2] - total) // 2
    found = jnp.zeros(ids.shape, F32)
    for k in range(n_e):
        pick = mine[k][0, :, total : total + 1].astype(F32) + mine[k][0, :, total + half : total + half + 1].astype(F32)
        hit = select[k * MOST : (k + 1) * MOST].astype(F32)
        value = jnp.sum(hit * pick, axis=0, keepdims=True)
        found = found + jnp.where(ids[...] == (e ^ k), value, 0.0)
    gate_grad[...] = (found / gates[...].astype(F32)).astype(BF16)


def call(kernel, args, places, outs, mib, scratch=(), places_out=None, hint=False, **static):
    args = [pltpu.with_memory_space_constraint(x, pltpu.HBM) if p == "h" else x for x, p in zip(args, places)]
    spaces = {"s": pltpu.SMEM, "v": pltpu.VMEM, "a": pl.ANY, "h": pltpu.HBM}
    return pl.pallas_call(
        functools.partial(kernel, **static),
        out_shape=outs,
        in_specs=[pl.BlockSpec(memory_space=spaces[p]) for p in places],
        **({"out_specs": pl.BlockSpec(memory_space=spaces[places_out])} if places_out else {}),
        scratch_shapes=scratch,
        **({"cost_estimate": HINT} if hint else {}),
        compiler_params=pltpu.CompilerParams(vmem_limit_bytes=mib * MIB),
    )(*args)


def after(x, *needs):
    return lax.optimization_barrier((x, *needs))[0] if needs else x


def to(x, position):
    n_f = lax.axis_size("fsdp")
    bits = n_f.bit_length() - 2
    return lax.ppermute(x, "fsdp", [(i, i ^ flips(position, i & 1, bits)) for i in range(n_f)])


def top(position):
    return 1 << (position.bit_length() - 1)


def per_device(tokens, out_grad, expert_ids, gate_probs, w_gate, w_up, w_down):
    tok, model = tokens.shape
    local, _, hidden = w_gate.shape
    n_f, n_e = lax.axis_size("fsdp"), lax.axis_size("ep")
    rows = n_e * MOST
    n = n_f // 2
    bits = n.bit_length() - 1
    near = [1 << b for b in range(bits)]
    late = [p for p in range(1, n) if p not in near]
    early = [0, *near]
    shape = jax.ShapeDtypeStruct

    weights = {
        0: call(
            stack_kernel,
            (w_gate[:, 0], w_up[:, 0], w_down[:, 0]),
            "hhh",
            shape((3 * local, hidden), BF16),
            8,
            [pltpu.SemaphoreType.DMA((3,))],
            places_out="a",
        )
    }
    for p in near:
        weights[p] = to(weights[0], p)

    pos = jnp.stack([lax.axis_index("fsdp"), lax.axis_index("ep")]).astype(jnp.int32)
    ids, gates = expert_ids.T, gate_probs.T
    *sends, select = call(
        prep_kernel,
        (pos, ids, gates, tokens, out_grad),
        "svvhh",
        [shape((2, 2 * MOST, model // 2), BF16)] * n_e + [shape((rows, tok), BF16)],
        16,
        [pltpu.VMEM(tokens.shape, BF16)] * 2 + [pltpu.SemaphoreType.DMA((2,))],
        n_f=n_f,
        n_e=n_e,
    )
    mine = [sends[0]] + [hop(sends[k], "ep", k) for k in range(1, n_e)]
    other = [hop(after(mine[0], weights[near[-1]]), "fsdp", 1)] + [hop(m, "fsdp", 1) for m in mine[1:]]
    both = (*mine, *other)
    for p in late:
        weights[p] = to(after(weights[p ^ top(p)], mine[1]), top(p))

    packed = call(pack_kernel, both, "v" * 2 * n_e, [shape((2, 2 * rows, local), BF16)] * (n - 1), 16, hint=True, n_e=n_e)
    got = [to(x, i + 1) for i, x in enumerate(packed)]

    def forward(entries, carried):
        pieces = [weights[p] for p in entries]
        size = len(entries) * local
        return call(
            forward_kernel,
            (*both, *carried, *pieces),
            "v" * (2 * n_e + len(carried)) + "a" * len(pieces),
            [shape((rows, 3 * hidden), F32), shape((rows, 3 * hidden), BF16)]
            if carried
            else [shape((2 * rows, 3 * hidden), F32)],
            24,
            [pltpu.VMEM((size, hidden), BF16)] * 3 + [pltpu.SemaphoreType.DMA((3 * len(entries),))],
            n_e=n_e,
            entries=entries,
            carried=bool(carried),
        )

    part = forward(early, ())[0]
    own, theirs = forward(late, [after(part, *got)])
    deltas0, pick = call(
        delta_kernel, (own, hop(theirs, "fsdp", 1)), "vv", [shape((rows, 3 * hidden), BF16), shape((rows, 128), BF16)], 16
    )
    deltas = {0: deltas0}
    for p in near:
        deltas[p] = to(deltas0, p)
    deltas_other = {0: hop(deltas0, "fsdp", 1)}

    backs = call(
        back_kernel,
        (deltas[0], deltas_other[0], pick, *(weights[p] for p in range(n))),
        "vvv" + "a" * n,
        [shape((2, MOST, model // 2 + 128), BF16)] * n_e,
        16,
        [pltpu.VMEM((n, local, hidden), BF16)] * 2 + [pltpu.SemaphoreType.DMA((2 * n,))],
        n=n,
        n_e=n_e,
    )
    back = [backs[0]] + [hop(backs[k], "ep", k) for k in range(1, n_e)]
    for p in late:
        deltas[p] = to(after(deltas[p ^ top(p)], back[1]), top(p))
    for p in near:
        deltas_other[p] = hop(after(deltas[p], *back[1:3]), "fsdp", 1)

    def weight_sums(entries, carried):
        far = [got[p - 1] for p in entries if p]
        parts = [x for p in entries for x in (deltas[p], deltas_other[mirror(p, bits)])]
        size = 2 * rows * len(entries)
        here = both if 0 in entries else ()
        return call(
            weight_kernel,
            (*here, *carried, *far, *parts),
            "v" * (len(here) + len(carried)) + "a" * (len(far) + len(parts)),
            [shape((local, hidden), BF16)] * 3 if carried else [shape((local, 3 * hidden), F32)],
            24,
            [pltpu.VMEM((size, local), BF16)] * 2
            + [pltpu.VMEM((size, 3 * hidden), BF16), pltpu.SemaphoreType.DMA((4 * len(far) + len(parts),))],
            n_e=n_e,
            entries=entries,
            carried=bool(carried),
        )

    part = weight_sums(early, ())[0]
    back_other = [hop(after(x, part) if k == n_e - 1 else x, "fsdp", 1) for k, x in enumerate(back)]
    in_grad, gate_grad = call(
        final_kernel,
        (pos, ids, gates, select, *back, *back_other),
        "svvv" + "v" * 2 * n_e,
        [shape((tok, model), BF16), shape(ids.shape, BF16)],
        16,
        n_f=n_f,
        n_e=n_e,
    )

    for p in late:
        deltas_other[p] = hop(after(deltas[p], part, *back_other), "fsdp", 1)
    grads = weight_sums(late, [after(part, in_grad)])
    return (in_grad, gate_grad.T, *(g[:, None] for g in grads))


def solution(mesh):
    tok = P(("fsdp", "ep"), None)
    weight = P("fsdp", "ep", None)
    return jax.shard_map(
        per_device,
        mesh=mesh,
        in_specs=(tok, tok, tok, tok, weight, weight, weight),
        out_specs=(tok, tok, weight, weight, weight),
        check_vma=False,
    )
```

```python
import functools
import itertools

import jax
import jax.numpy as jnp
from jax import lax
from jax.experimental import pallas as pl
from jax.experimental.pallas import tpu as pltpu
from jax.sharding import PartitionSpec as P

MOST = 32
F32 = jnp.float32
BF16 = jnp.bfloat16
MIB = 1024 * 1024
HINT = pl.CostEstimate(flops=5_000_000_000, bytes_accessed=15_000_000, transcendentals=0)


def mm(left, right):
    return lax.dot_general(left, right, (((1,), (0,)), ((), ())), preferred_element_type=F32)


def mm_lead(left, right):
    return lax.dot_general(left, right, (((0,), (0,)), ((), ())), preferred_element_type=F32)


def mm_trail(left, right):
    return lax.dot_general(left, right, (((1,), (1,)), ((), ())), preferred_element_type=F32)


def hop(x, axis, offset):
    return lax.ppermute(x, axis, [(i, i ^ offset) for i in range(lax.axis_size(axis))])


def flips(position, core, bits):
    return sum(2 << (bits - 1 - b if core else b) for b in range(bits) if position >> b & 1)


def mirror(position, bits):
    return flips(position, 1, bits) // 2


def slice_of(f, side, position, n_f):
    bits = n_f.bit_length() - 2
    even, odd = flips(position, 0, bits), flips(position, 1, bits)
    return f ^ side ^ (even + ((f ^ side) & 1) * (odd - even))


class Copies:
    def __init__(self, sems):
        self.sems, self.made, self.waited = sems, [], 0

    def start(self, source, target):
        self.made.append(pltpu.make_async_copy(source, target, self.sems.at[len(self.made)]))
        self.made[-1].start()

    def wait(self, count=None):
        for copy in self.made[self.waited : None if count is None else self.waited + count]:
            copy.wait()
            self.waited += 1


def stack_kernel(*refs):
    parts, (out, sems) = refs[:-2], refs[-2:]
    fetch = Copies(sems)
    size = parts[0].shape[0]
    for i, part in enumerate(parts):
        fetch.start(part, out.at[pl.ds(i * size, size)])
    fetch.wait()


def prep_kernel(pos, ids, gates, tokens_in, grads_in, *refs, n_f, n_e):
    sends, select = refs[:n_e], refs[n_e]
    tokens, grads, sems = refs[n_e + 1 :]
    fetch = [
        pltpu.make_async_copy(tokens_in, tokens, sems.at[0]),
        pltpu.make_async_copy(grads_in, grads, sems.at[1]),
    ]
    for copy in fetch:
        copy.start()
    f, e = pos[0], pos[1]
    tok = ids.shape[1]
    width = tokens.shape[1] // n_f
    rows = max(16, n_e)
    row = lax.broadcasted_iota(jnp.int32, (rows, tok), 0)
    chosen = []
    weight = []
    stacked = jnp.zeros((rows, tok), F32)
    for k in range(n_e):
        match = ids[...] == (e ^ k)
        chosen.append(jnp.max(jnp.where(match, 1.0, 0.0), axis=0, keepdims=True))
        weight.append(jnp.sum(jnp.where(match, gates[...].astype(F32), 0.0), axis=0, keepdims=True))
        stacked = jnp.where(row == k, chosen[k], stacked)
    before = lax.broadcasted_iota(jnp.int32, (tok, tok), 0) < lax.broadcasted_iota(jnp.int32, (tok, tok), 1)
    slot = mm(stacked.astype(BF16), jnp.where(before, 1.0, 0.0).astype(BF16))
    want = lax.broadcasted_iota(jnp.int32, (MOST, tok), 0).astype(F32)
    picks = []
    scaled = []
    for k in range(n_e):
        hit = jnp.where(want == slot[k : k + 1], chosen[k], 0.0)
        picks.append(hit)
        scaled.append(hit * weight[k])
    picks = jnp.concatenate(picks, axis=0).astype(BF16)
    scaled = jnp.concatenate(scaled, axis=0).astype(BF16)
    select[...] = picks
    for copy in fetch:
        copy.wait()
    for side, position in itertools.product(range(2), range(n_f // 2)):
        at = pl.ds(pl.multiple_of(slice_of(f, side, position, n_f) * width, width), width)
        here = slice(position * width, (position + 1) * width)
        x = mm(picks, tokens[:, at]).astype(BF16)
        q = mm(scaled, grads[:, at]).astype(BF16)
        for k in range(n_e):
            sends[k][side, :MOST, here] = x[k * MOST : (k + 1) * MOST]
            sends[k][side, MOST:, here] = q[k * MOST : (k + 1) * MOST]


def pack_kernel(*refs, n_e):
    sides = refs[:n_e], refs[n_e : 2 * n_e]
    outs = refs[2 * n_e :]
    width = outs[0].shape[2]
    rows = n_e * MOST
    for i, out in enumerate(outs):
        here = slice((i + 1) * width, (i + 2) * width)
        for side in range(2):
            for k in range(n_e):
                out[side, k * MOST : (k + 1) * MOST] = sides[side][k][side, :MOST, here]
                out[side, rows + k * MOST : rows + (k + 1) * MOST] = sides[side][k][side, MOST:, here]


def forward_kernel(*refs, n_e, entries, carried):
    sides = refs[:n_e], refs[n_e : 2 * n_e]
    refs = refs[2 * n_e :]
    if carried:
        total_in, refs = refs[0], refs[1:]
    count = len(entries)
    pieces, outs = refs[:count], refs[count:]
    width, hidden = pieces[0].shape[0] // 3, pieces[0].shape[1]

    def rows_of(part):
        return jnp.concatenate(
            [
                jnp.concatenate([sides[side][k][side, part, i * width : (i + 1) * width] for i in entries], axis=1)
                for side in range(2)
                for k in range(n_e)
            ],
            axis=0,
        )

    x, q = rows_of(slice(0, MOST)), rows_of(slice(MOST, 2 * MOST))
    rows = n_e * MOST
    for at, left in enumerate((x, x, q)):
        right = jnp.concatenate([p[at * width : (at + 1) * width] for p in pieces], axis=0)
        here = slice(at * hidden, (at + 1) * hidden)
        part = mm(left, right)
        if carried:
            part = part + total_in[:, here]
            outs[0][:, here] = part[:rows]
            outs[1][:, here] = part[rows:].astype(BF16)
        else:
            outs[0][:, here] = part


def delta_kernel(own, got, deltas, pick_out):
    hidden = own.shape[1] // 3
    a, b, r = (
        own[:, at * hidden : (at + 1) * hidden] + got[:, at * hidden : (at + 1) * hidden].astype(F32) for at in range(3)
    )
    s = jax.nn.sigmoid(a)
    silu = a * s
    h = (silu * b).astype(BF16)
    pick = jnp.sum(h.astype(F32) * r, axis=1, keepdims=True)
    deltas[:, :hidden] = (r * b * s * (1.0 + a * (1.0 - s))).astype(BF16)
    deltas[:, hidden : 2 * hidden] = (r * silu).astype(BF16)
    deltas[:, 2 * hidden :] = h
    coarse = pick.astype(BF16)
    fine = (pick - coarse.astype(F32)).astype(BF16)
    wide = pick_out.shape
    lane = lax.broadcasted_iota(jnp.int32, wide, 1)
    pick_out[...] = jnp.where(
        lane < wide[1] // 2, jnp.broadcast_to(coarse.astype(F32), wide), jnp.broadcast_to(fine.astype(F32), wide)
    ).astype(BF16)


def back_kernel(deltas, deltas_other, pick, *refs, n, n_e):
    pieces, outs = refs[:n], refs[n:]
    width, hidden = pieces[0].shape[0] // 3, pieces[0].shape[1]
    da = jnp.concatenate([deltas[:, :hidden], deltas_other[:, :hidden]], axis=0)
    du = jnp.concatenate([deltas[:, hidden : 2 * hidden], deltas_other[:, hidden : 2 * hidden]], axis=0)
    for i in range(n):
        c = (mm_trail(da, pieces[i][:width]) + mm_trail(du, pieces[i][width : 2 * width])).astype(BF16)
        here = slice(i * width, (i + 1) * width)
        for side in range(2):
            for k in range(n_e):
                at = (side * n_e + k) * MOST
                outs[k][side, :, here] = c[at : at + MOST]
    for side in range(2):
        for k in range(n_e):
            outs[k][side, :, n * width :] = pick[k * MOST : (k + 1) * MOST]


def weight_kernel(*refs, n_e, count, entries, carried):
    if 0 in entries:
        sides, refs = (refs[:n_e], refs[n_e : 2 * n_e]), refs[2 * n_e :]
    if carried:
        total_in, refs = refs[0], refs[1:]
    far = [i for i in entries if i]
    got, deltas = refs[: len(far)], refs[len(far) : len(far) + 2 * len(entries)]
    outs = refs[len(far) + 2 * len(entries) :]
    hidden = deltas[0].shape[1] // 3
    rows = n_e * MOST

    def rows_of(part):
        lefts = []
        for i in entries:
            for side in range(2):
                if i:
                    lefts.append(got[far.index(i)][side, part * rows : (part + 1) * rows])
                else:
                    width = sides[0][0].shape[2] // count
                    lefts += [s[side, part * MOST : (part + 1) * MOST, :width] for s in sides[side]]
        return jnp.concatenate(lefts, axis=0)

    x, q = rows_of(0), rows_of(1)
    for at, left in enumerate((x, x, q)):
        here = slice(at * hidden, (at + 1) * hidden)
        part = mm_lead(left, jnp.concatenate([d[:, here] for d in deltas], axis=0))
        if carried:
            outs[at][...] = (total_in[:, here] + part).astype(BF16)
        else:
            outs[0][:, here] = part


def final_kernel(pos, ids, gates, select, *refs, n_f, n_e):
    mine, other, (in_grad, gate_grad) = refs[:n_e], refs[n_e : 2 * n_e], refs[2 * n_e :]
    f, e = pos[0], pos[1]
    width = in_grad.shape[1] // n_f
    total = n_f // 2 * width
    for side in range(2):
        c = jnp.concatenate([(mine, other)[side][k][side, :, :total] for k in range(n_e)], axis=0)
        rows = mm_lead(select[...], c).astype(BF16)
        for position in range(n_f // 2):
            at = pl.ds(pl.multiple_of(slice_of(f, side, position, n_f) * width, width), width)
            in_grad[:, at] = rows[:, position * width : (position + 1) * width]
    half = (mine[0].shape[2] - total) // 2
    found = jnp.zeros(ids.shape, F32)
    for k in range(n_e):
        pick = mine[k][0, :, total : total + 1].astype(F32) + mine[k][0, :, total + half : total + half + 1].astype(F32)
        hit = select[k * MOST : (k + 1) * MOST].astype(F32)
        value = jnp.sum(hit * pick, axis=0, keepdims=True)
        found = found + jnp.where(ids[...] == (e ^ k), value, 0.0)
    gate_grad[...] = (found / gates[...].astype(F32)).astype(BF16)


def call(kernel, args, places, outs, mib, scratch=(), places_out=None, hint=False, **static):
    args = [pltpu.with_memory_space_constraint(x, pltpu.HBM) if p == "h" else x for x, p in zip(args, places)]
    spaces = {"s": pltpu.SMEM, "v": pltpu.VMEM, "a": pl.ANY, "h": pltpu.HBM}
    return pl.pallas_call(
        functools.partial(kernel, **static),
        out_shape=outs,
        in_specs=[pl.BlockSpec(memory_space=spaces[p]) for p in places],
        **({"out_specs": pl.BlockSpec(memory_space=spaces[places_out])} if places_out else {}),
        scratch_shapes=scratch,
        **({"cost_estimate": HINT} if hint else {}),
        compiler_params=pltpu.CompilerParams(vmem_limit_bytes=mib * MIB),
    )(*args)


def after(x, *needs):
    return lax.optimization_barrier((x, *needs))[0] if needs else x


def to(x, position):
    n_f = lax.axis_size("fsdp")
    bits = n_f.bit_length() - 2
    return lax.ppermute(x, "fsdp", [(i, i ^ flips(position, i & 1, bits)) for i in range(n_f)])


def top(position):
    return 1 << (position.bit_length() - 1)


def per_device(tokens, out_grad, expert_ids, gate_probs, w_gate, w_up, w_down):
    tok, model = tokens.shape
    local, _, hidden = w_gate.shape
    n_f, n_e = lax.axis_size("fsdp"), lax.axis_size("ep")
    rows = n_e * MOST
    n = n_f // 2
    bits = n.bit_length() - 1
    near = [1 << b for b in range(bits)]
    late = [p for p in range(1, n) if p not in near]
    early = [0, *near]
    shape = jax.ShapeDtypeStruct

    weights = {
        0: call(
            stack_kernel,
            (w_gate[:, 0], w_up[:, 0], w_down[:, 0]),
            "hhh",
            shape((3 * local, hidden), BF16),
            8,
            [pltpu.SemaphoreType.DMA((3,))],
            places_out="a",
        )
    }
    for p in near:
        weights[p] = to(weights[0], p)

    pos = jnp.stack([lax.axis_index("fsdp"), lax.axis_index("ep")]).astype(jnp.int32)
    ids, gates = expert_ids.T, gate_probs.T
    *sends, select = call(
        prep_kernel,
        (pos, ids, gates, tokens, out_grad),
        "svvhh",
        [shape((2, 2 * MOST, model // 2), BF16)] * n_e + [shape((rows, tok), BF16)],
        16,
        [pltpu.VMEM(tokens.shape, BF16)] * 2 + [pltpu.SemaphoreType.DMA((2,))],
        n_f=n_f,
        n_e=n_e,
    )
    mine = [sends[0]] + [hop(sends[k], "ep", k) for k in range(1, n_e)]
    other = [hop(after(mine[0], weights[near[-1]]), "fsdp", 1)] + [hop(m, "fsdp", 1) for m in mine[1:]]
    both = (*mine, *other)
    for p in late:
        weights[p] = to(after(weights[p ^ top(p)], mine[1]), top(p))

    packed = call(pack_kernel, both, "v" * 2 * n_e, [shape((2, 2 * rows, local), BF16)] * (n - 1), 16, hint=True, n_e=n_e)
    got = [to(x, i + 1) for i, x in enumerate(packed)]

    def forward(entries, carried):
        pieces = [weights[p] for p in entries]
        return call(
            forward_kernel,
            (*both, *carried, *pieces),
            "v" * (2 * n_e + len(carried) + len(pieces)),
            [shape((rows, 3 * hidden), F32), shape((rows, 3 * hidden), BF16)]
            if carried
            else [shape((2 * rows, 3 * hidden), F32)],
            32,
            n_e=n_e,
            entries=entries,
            carried=bool(carried),
        )

    part = forward(early, ())[0]
    own, theirs = forward(late, [after(part, got[0])])
    deltas0, pick = call(
        delta_kernel, (own, hop(theirs, "fsdp", 1)), "vv", [shape((rows, 3 * hidden), BF16), shape((rows, 128), BF16)], 16
    )
    deltas = {0: deltas0}
    for p in near:
        deltas[p] = to(deltas0, p)
    deltas_other = {0: hop(deltas0, "fsdp", 1)}

    backs = call(
        back_kernel,
        (deltas[0], deltas_other[0], pick, *(weights[p] for p in range(n))),
        "v" * (3 + n),
        [shape((2, MOST, model // 2 + 128), BF16)] * n_e,
        24,
        n=n,
        n_e=n_e,
    )
    back = [backs[0]] + [hop(backs[k], "ep", k) for k in range(1, n_e)]
    for p in late:
        deltas[p] = to(after(deltas[p ^ top(p)], back[1], *got[1:-1]), top(p))
    for p in near:
        deltas_other[p] = hop(after(deltas[p], *back[1:3]), "fsdp", 1)

    def weight_sums(entries, carried):
        far = [got[p - 1] for p in entries if p]
        parts = [x for p in entries for x in (deltas[p], deltas_other[mirror(p, bits)])]
        here = both if 0 in entries else ()
        return call(
            weight_kernel,
            (*here, *carried, *far, *parts),
            "v" * (len(here) + len(carried) + len(far) + len(parts)),
            [shape((local, hidden), BF16)] * 3 if carried else [shape((local, 3 * hidden), F32)],
            32,
            count=n,
            n_e=n_e,
            entries=entries,
            carried=bool(carried),
        )

    part = weight_sums(early, ())[0]
    back_other = [hop(after(x, part, got[-1]) if k == n_e - 1 else x, "fsdp", 1) for k, x in enumerate(back)]
    in_grad, gate_grad = call(
        final_kernel,
        (pos, ids, gates, select, *back, *back_other),
        "svvv" + "v" * 2 * n_e,
        [shape((tok, model), BF16), shape(ids.shape, BF16)],
        16,
        n_f=n_f,
        n_e=n_e,
    )

    for p in late:
        deltas_other[p] = hop(after(deltas[p], part, *back_other), "fsdp", 1)
    grads = weight_sums(late, [after(part, in_grad)])
    return (in_grad, gate_grad.T, *(g[:, None] for g in grads))


def solution(mesh):
    tok = P(("fsdp", "ep"), None)
    weight = P("fsdp", "ep", None)
    return jax.shard_map(
        per_device,
        mesh=mesh,
        in_specs=(tok, tok, tok, tok, weight, weight, weight),
        out_specs=(tok, tok, weight, weight, weight),
        check_vma=False,
    )
```

```python
import functools
import itertools

import jax
import jax.numpy as jnp
from jax import lax
from jax.experimental import pallas as pl
from jax.experimental.pallas import tpu as pltpu
from jax.sharding import PartitionSpec as P

MOST = 32
F32 = jnp.float32
BF16 = jnp.bfloat16
MIB = 1024 * 1024
HINT = pl.CostEstimate(flops=5_000_000_000, bytes_accessed=15_000_000, transcendentals=0)


def mm(left, right):
    return lax.dot_general(left, right, (((1,), (0,)), ((), ())), preferred_element_type=F32)


def mm_lead(left, right):
    return lax.dot_general(left, right, (((0,), (0,)), ((), ())), preferred_element_type=F32)


def mm_trail(left, right):
    return lax.dot_general(left, right, (((1,), (1,)), ((), ())), preferred_element_type=F32)


def hop(x, axis, offset):
    return lax.ppermute(x, axis, [(i, i ^ offset) for i in range(lax.axis_size(axis))])


def flips(position, core, bits):
    return sum(2 << (bits - 1 - b if core else b) for b in range(bits) if position >> b & 1)


def mirror(position, bits):
    return flips(position, 1, bits) // 2


def slice_of(f, side, position, n_f):
    bits = n_f.bit_length() - 2
    even, odd = flips(position, 0, bits), flips(position, 1, bits)
    return f ^ side ^ (even + ((f ^ side) & 1) * (odd - even))


class Copies:
    def __init__(self, sems):
        self.sems, self.made, self.waited = sems, [], 0

    def start(self, source, target):
        self.made.append(pltpu.make_async_copy(source, target, self.sems.at[len(self.made)]))
        self.made[-1].start()

    def wait(self, count=None):
        for copy in self.made[self.waited : None if count is None else self.waited + count]:
            copy.wait()
            self.waited += 1


def stack_kernel(*refs):
    parts, (out, sems) = refs[:-2], refs[-2:]
    fetch = Copies(sems)
    size = parts[0].shape[0]
    for i, part in enumerate(parts):
        fetch.start(part, out.at[pl.ds(i * size, size)])
    fetch.wait()


def prep_kernel(pos, ids, gates, tokens_in, grads_in, *refs, n_f, n_e):
    sends, select = refs[:n_e], refs[n_e]
    tokens, grads, sems = refs[n_e + 1 :]
    fetch = [
        pltpu.make_async_copy(tokens_in, tokens, sems.at[0]),
        pltpu.make_async_copy(grads_in, grads, sems.at[1]),
    ]
    for copy in fetch:
        copy.start()
    f, e = pos[0], pos[1]
    tok = ids.shape[1]
    width = tokens.shape[1] // n_f
    rows = max(16, n_e)
    row = lax.broadcasted_iota(jnp.int32, (rows, tok), 0)
    chosen = []
    weight = []
    stacked = jnp.zeros((rows, tok), F32)
    for k in range(n_e):
        match = ids[...] == (e ^ k)
        chosen.append(jnp.max(jnp.where(match, 1.0, 0.0), axis=0, keepdims=True))
        weight.append(jnp.sum(jnp.where(match, gates[...].astype(F32), 0.0), axis=0, keepdims=True))
        stacked = jnp.where(row == k, chosen[k], stacked)
    before = lax.broadcasted_iota(jnp.int32, (tok, tok), 0) < lax.broadcasted_iota(jnp.int32, (tok, tok), 1)
    slot = mm(stacked.astype(BF16), jnp.where(before, 1.0, 0.0).astype(BF16))
    want = lax.broadcasted_iota(jnp.int32, (MOST, tok), 0).astype(F32)
    picks = []
    scaled = []
    for k in range(n_e):
        hit = jnp.where(want == slot[k : k + 1], chosen[k], 0.0)
        picks.append(hit)
        scaled.append(hit * weight[k])
    picks = jnp.concatenate(picks, axis=0).astype(BF16)
    scaled = jnp.concatenate(scaled, axis=0).astype(BF16)
    select[...] = picks
    for copy in fetch:
        copy.wait()
    for side, position in itertools.product(range(2), range(n_f // 2)):
        at = pl.ds(pl.multiple_of(slice_of(f, side, position, n_f) * width, width), width)
        here = slice(position * width, (position + 1) * width)
        x = mm(picks, tokens[:, at]).astype(BF16)
        q = mm(scaled, grads[:, at]).astype(BF16)
        for k in range(n_e):
            sends[k][side, :MOST, here] = x[k * MOST : (k + 1) * MOST]
            sends[k][side, MOST:, here] = q[k * MOST : (k + 1) * MOST]


def pack_kernel(*refs, n_e):
    sides = refs[:n_e], refs[n_e : 2 * n_e]
    outs = refs[2 * n_e :]
    width = outs[0].shape[2]
    rows = n_e * MOST
    for i, out in enumerate(outs):
        here = slice((i + 1) * width, (i + 2) * width)
        for side in range(2):
            for k in range(n_e):
                out[side, k * MOST : (k + 1) * MOST] = sides[side][k][side, :MOST, here]
                out[side, rows + k * MOST : rows + (k + 1) * MOST] = sides[side][k][side, MOST:, here]


def forward_kernel(*refs, n_e, entries, carried):
    sides = refs[:n_e], refs[n_e : 2 * n_e]
    refs = refs[2 * n_e :]
    if carried:
        total_in, refs = refs[0], refs[1:]
    count = len(entries)
    pieces, outs = refs[:count], refs[count:]
    width, hidden = pieces[0].shape[0] // 3, pieces[0].shape[1]

    def rows_of(part):
        return jnp.concatenate(
            [
                jnp.concatenate([sides[side][k][side, part, i * width : (i + 1) * width] for i in entries], axis=1)
                for side in range(2)
                for k in range(n_e)
            ],
            axis=0,
        )

    x, q = rows_of(slice(0, MOST)), rows_of(slice(MOST, 2 * MOST))
    rows = n_e * MOST
    for at, left in enumerate((x, x, q)):
        right = jnp.concatenate([p[at * width : (at + 1) * width] for p in pieces], axis=0)
        here = slice(at * hidden, (at + 1) * hidden)
        part = mm(left, right)
        if carried:
            part = part + total_in[:, here]
            outs[0][:, here] = part[:rows]
            outs[1][:, here] = part[rows:].astype(BF16)
        else:
            outs[0][:, here] = part


def delta_kernel(own, got, deltas, pick_out):
    hidden = own.shape[1] // 3
    a, b, r = (
        own[:, at * hidden : (at + 1) * hidden] + got[:, at * hidden : (at + 1) * hidden].astype(F32) for at in range(3)
    )
    s = jax.nn.sigmoid(a)
    silu = a * s
    h = (silu * b).astype(BF16)
    pick = jnp.sum(h.astype(F32) * r, axis=1, keepdims=True)
    deltas[:, :hidden] = (r * b * s * (1.0 + a * (1.0 - s))).astype(BF16)
    deltas[:, hidden : 2 * hidden] = (r * silu).astype(BF16)
    deltas[:, 2 * hidden :] = h
    coarse = pick.astype(BF16)
    fine = (pick - coarse.astype(F32)).astype(BF16)
    wide = pick_out.shape
    lane = lax.broadcasted_iota(jnp.int32, wide, 1)
    pick_out[...] = jnp.where(
        lane < wide[1] // 2, jnp.broadcast_to(coarse.astype(F32), wide), jnp.broadcast_to(fine.astype(F32), wide)
    ).astype(BF16)


def back_kernel(deltas, deltas_other, pick, *refs, n, n_e):
    pieces, outs = refs[:n], refs[n:]
    width, hidden = pieces[0].shape[0] // 3, pieces[0].shape[1]
    da = jnp.concatenate([deltas[:, :hidden], deltas_other[:, :hidden]], axis=0)
    du = jnp.concatenate([deltas[:, hidden : 2 * hidden], deltas_other[:, hidden : 2 * hidden]], axis=0)
    for i in range(n):
        c = (mm_trail(da, pieces[i][:width]) + mm_trail(du, pieces[i][width : 2 * width])).astype(BF16)
        here = slice(i * width, (i + 1) * width)
        for side in range(2):
            for k in range(n_e):
                at = (side * n_e + k) * MOST
                outs[k][side, :, here] = c[at : at + MOST]
    for side in range(2):
        for k in range(n_e):
            outs[k][side, :, n * width :] = pick[k * MOST : (k + 1) * MOST]


def weight_kernel(*refs, n_e, count, entries, carried):
    if 0 in entries:
        sides, refs = (refs[:n_e], refs[n_e : 2 * n_e]), refs[2 * n_e :]
    if carried:
        total_in, refs = refs[0], refs[1:]
    far = [i for i in entries if i]
    got, deltas = refs[: len(far)], refs[len(far) : len(far) + 2 * len(entries)]
    outs = refs[len(far) + 2 * len(entries) :]
    hidden = deltas[0].shape[1] // 3
    rows = n_e * MOST

    def rows_of(part):
        lefts = []
        for i in entries:
            for side in range(2):
                if i:
                    lefts.append(got[far.index(i)][side, part * rows : (part + 1) * rows])
                else:
                    width = sides[0][0].shape[2] // count
                    lefts += [s[side, part * MOST : (part + 1) * MOST, :width] for s in sides[side]]
        return jnp.concatenate(lefts, axis=0)

    x, q = rows_of(0), rows_of(1)
    for at, left in enumerate((x, x, q)):
        here = slice(at * hidden, (at + 1) * hidden)
        part = mm_lead(left, jnp.concatenate([d[:, here] for d in deltas], axis=0))
        if carried:
            outs[at][...] = (total_in[:, here] + part).astype(BF16)
        else:
            outs[0][:, here] = part


def final_kernel(pos, ids, gates, select, *refs, n_f, n_e):
    mine, other, (in_grad, gate_grad) = refs[:n_e], refs[n_e : 2 * n_e], refs[2 * n_e :]
    f, e = pos[0], pos[1]
    width = in_grad.shape[1] // n_f
    total = n_f // 2 * width
    for side in range(2):
        c = jnp.concatenate([(mine, other)[side][k][side, :, :total] for k in range(n_e)], axis=0)
        rows = mm_lead(select[...], c).astype(BF16)
        for position in range(n_f // 2):
            at = pl.ds(pl.multiple_of(slice_of(f, side, position, n_f) * width, width), width)
            in_grad[:, at] = rows[:, position * width : (position + 1) * width]
    half = (mine[0].shape[2] - total) // 2
    found = jnp.zeros(ids.shape, F32)
    for k in range(n_e):
        pick = mine[k][0, :, total : total + 1].astype(F32) + mine[k][0, :, total + half : total + half + 1].astype(F32)
        hit = select[k * MOST : (k + 1) * MOST].astype(F32)
        value = jnp.sum(hit * pick, axis=0, keepdims=True)
        found = found + jnp.where(ids[...] == (e ^ k), value, 0.0)
    gate_grad[...] = (found / gates[...].astype(F32)).astype(BF16)


def call(kernel, args, places, outs, mib, scratch=(), places_out=None, hint=False, **static):
    args = [pltpu.with_memory_space_constraint(x, pltpu.HBM) if p == "h" else x for x, p in zip(args, places)]
    spaces = {"s": pltpu.SMEM, "v": pltpu.VMEM, "a": pl.ANY, "h": pltpu.HBM}
    return pl.pallas_call(
        functools.partial(kernel, **static),
        out_shape=outs,
        in_specs=[pl.BlockSpec(memory_space=spaces[p]) for p in places],
        **({"out_specs": pl.BlockSpec(memory_space=spaces[places_out])} if places_out else {}),
        scratch_shapes=scratch,
        **({"cost_estimate": HINT} if hint else {}),
        compiler_params=pltpu.CompilerParams(vmem_limit_bytes=mib * MIB),
    )(*args)


def after(x, *needs):
    return lax.optimization_barrier((x, *needs))[0] if needs else x


def to(x, position):
    n_f = lax.axis_size("fsdp")
    bits = n_f.bit_length() - 2
    return lax.ppermute(x, "fsdp", [(i, i ^ flips(position, i & 1, bits)) for i in range(n_f)])


def top(position):
    return 1 << (position.bit_length() - 1)


def per_device(tokens, out_grad, expert_ids, gate_probs, w_gate, w_up, w_down):
    tok, model = tokens.shape
    local, _, hidden = w_gate.shape
    n_f, n_e = lax.axis_size("fsdp"), lax.axis_size("ep")
    rows = n_e * MOST
    n = n_f // 2
    bits = n.bit_length() - 1
    near = [1 << b for b in range(bits)]
    late = [p for p in range(1, n) if p not in near]
    early = [0, *near]
    shape = jax.ShapeDtypeStruct

    weights = {
        0: call(
            stack_kernel,
            (w_gate[:, 0], w_up[:, 0], w_down[:, 0]),
            "hhh",
            shape((3 * local, hidden), BF16),
            8,
            [pltpu.SemaphoreType.DMA((3,))],
            places_out="a",
        )
    }
    for p in near:
        weights[p] = to(weights[0], p)

    pos = jnp.stack([lax.axis_index("fsdp"), lax.axis_index("ep")]).astype(jnp.int32)
    ids, gates = expert_ids.T, gate_probs.T
    *sends, select = call(
        prep_kernel,
        (pos, ids, gates, tokens, out_grad),
        "svvhh",
        [shape((2, 2 * MOST, model // 2), BF16)] * n_e + [shape((rows, tok), BF16)],
        16,
        [pltpu.VMEM(tokens.shape, BF16)] * 2 + [pltpu.SemaphoreType.DMA((2,))],
        n_f=n_f,
        n_e=n_e,
    )
    mine = [sends[0]] + [hop(sends[k], "ep", k) for k in range(1, n_e)]
    other = [hop(after(mine[0], weights[near[-1]]), "fsdp", 1)] + [hop(m, "fsdp", 1) for m in mine[1:]]
    both = (*mine, *other)
    for p in late:
        weights[p] = to(after(weights[p ^ top(p)], mine[1]), top(p))

    packed = call(pack_kernel, both, "v" * 2 * n_e, [shape((2, 2 * rows, local), BF16)] * (n - 1), 16, hint=True, n_e=n_e)
    got = [to(x, i + 1) for i, x in enumerate(packed)]

    def forward(entries, carried):
        pieces = [weights[p] for p in entries]
        return call(
            forward_kernel,
            (*both, *carried, *pieces),
            "v" * (2 * n_e + len(carried) + len(pieces)),
            [shape((rows, 3 * hidden), F32), shape((rows, 3 * hidden), BF16)]
            if carried
            else [shape((2 * rows, 3 * hidden), F32)],
            32,
            n_e=n_e,
            entries=entries,
            carried=bool(carried),
        )

    part = forward(early, ())[0]
    own, theirs = forward(late, [after(part, got[0])])
    deltas0, pick = call(
        delta_kernel, (own, hop(theirs, "fsdp", 1)), "vv", [shape((rows, 3 * hidden), BF16), shape((rows, 128), BF16)], 16
    )
    deltas = {0: deltas0}
    for p in near:
        deltas[p] = to(deltas0, p)
    deltas_other = {0: hop(deltas0, "fsdp", 1)}

    backs = call(
        back_kernel,
        (deltas[0], deltas_other[0], pick, *(weights[p] for p in range(n))),
        "v" * (3 + n),
        [shape((2, MOST, model // 2 + 128), BF16)] * n_e,
        24,
        n=n,
        n_e=n_e,
    )
    back = [backs[0]] + [hop(backs[k], "ep", k) for k in range(1, n_e)]
    for p in late:
        deltas[p] = to(after(deltas[p ^ top(p)], back[1], *got[1:-1]), top(p))
    for p in near:
        deltas_other[p] = hop(after(deltas[p], *back[1:3]), "fsdp", 1)

    def weight_sums(entries, carried):
        far = [got[p - 1] for p in entries if p]
        parts = [x for p in entries for x in (deltas[p], deltas_other[mirror(p, bits)])]
        here = both if 0 in entries else ()
        return call(
            weight_kernel,
            (*here, *carried, *far, *parts),
            "v" * (len(here) + len(carried) + len(far) + len(parts)),
            [shape((local, hidden), BF16)] * 3 if carried else [shape((local, 3 * hidden), F32)],
            32,
            count=n,
            n_e=n_e,
            entries=entries,
            carried=bool(carried),
        )

    part = weight_sums(early, ())[0]
    back_other = [hop(after(x, part) if k == n_e - 1 else x, "fsdp", 1) for k, x in enumerate(back)]
    in_grad, gate_grad = call(
        final_kernel,
        (pos, ids, gates, select, *back, *back_other),
        "svvv" + "v" * 2 * n_e,
        [shape((tok, model), BF16), shape(ids.shape, BF16)],
        16,
        n_f=n_f,
        n_e=n_e,
    )

    for p in late:
        deltas_other[p] = hop(after(deltas[p], part, in_grad, got[-1]), "fsdp", 1)
    grads = weight_sums(late, [part])
    return (in_grad, gate_grad.T, *(g[:, None] for g in grads))


def solution(mesh):
    tok = P(("fsdp", "ep"), None)
    weight = P("fsdp", "ep", None)
    return jax.shard_map(
        per_device,
        mesh=mesh,
        in_specs=(tok, tok, tok, tok, weight, weight, weight),
        out_specs=(tok, tok, weight, weight, weight),
        check_vma=False,
    )
```

```python
import functools
import itertools

import jax
import jax.numpy as jnp
from jax import lax
from jax.experimental import pallas as pl
from jax.experimental.pallas import tpu as pltpu
from jax.sharding import PartitionSpec as P

MOST = 32
F32 = jnp.float32
BF16 = jnp.bfloat16
MIB = 1024 * 1024
HINT = pl.CostEstimate(flops=5_000_000_000, bytes_accessed=15_000_000, transcendentals=0)


def mm(left, right):
    return lax.dot_general(left, right, (((1,), (0,)), ((), ())), preferred_element_type=F32)


def mm_lead(left, right):
    return lax.dot_general(left, right, (((0,), (0,)), ((), ())), preferred_element_type=F32)


def mm_trail(left, right):
    return lax.dot_general(left, right, (((1,), (1,)), ((), ())), preferred_element_type=F32)


def hop(x, axis, offset):
    return lax.ppermute(x, axis, [(i, i ^ offset) for i in range(lax.axis_size(axis))])


def flips(position, core, bits):
    return sum(2 << (bits - 1 - b if core else b) for b in range(bits) if position >> b & 1)


def mirror(position, bits):
    return flips(position, 1, bits) // 2


def slice_of(f, side, position, n_f):
    bits = n_f.bit_length() - 2
    even, odd = flips(position, 0, bits), flips(position, 1, bits)
    return f ^ side ^ (even + ((f ^ side) & 1) * (odd - even))


class Copies:
    def __init__(self, sems):
        self.sems, self.made, self.waited = sems, [], 0

    def start(self, source, target):
        self.made.append(pltpu.make_async_copy(source, target, self.sems.at[len(self.made)]))
        self.made[-1].start()

    def wait(self, count=None):
        for copy in self.made[self.waited : None if count is None else self.waited + count]:
            copy.wait()
            self.waited += 1


def stack_kernel(*refs):
    parts, (out, sems) = refs[:-2], refs[-2:]
    fetch = Copies(sems)
    size = parts[0].shape[0]
    for i, part in enumerate(parts):
        fetch.start(part, out.at[pl.ds(i * size, size)])
    fetch.wait()


def prep_kernel(pos, ids, gates, tokens_in, grads_in, *refs, n_f, n_e):
    sends, select = refs[:n_e], refs[n_e]
    tokens, grads, sems = refs[n_e + 1 :]
    fetch = [
        pltpu.make_async_copy(tokens_in, tokens, sems.at[0]),
        pltpu.make_async_copy(grads_in, grads, sems.at[1]),
    ]
    for copy in fetch:
        copy.start()
    f, e = pos[0], pos[1]
    tok = ids.shape[1]
    width = tokens.shape[1] // n_f
    rows = max(16, n_e)
    row = lax.broadcasted_iota(jnp.int32, (rows, tok), 0)
    chosen = []
    weight = []
    stacked = jnp.zeros((rows, tok), F32)
    for k in range(n_e):
        match = ids[...] == (e ^ k)
        chosen.append(jnp.max(jnp.where(match, 1.0, 0.0), axis=0, keepdims=True))
        weight.append(jnp.sum(jnp.where(match, gates[...].astype(F32), 0.0), axis=0, keepdims=True))
        stacked = jnp.where(row == k, chosen[k], stacked)
    before = lax.broadcasted_iota(jnp.int32, (tok, tok), 0) < lax.broadcasted_iota(jnp.int32, (tok, tok), 1)
    slot = mm(stacked.astype(BF16), jnp.where(before, 1.0, 0.0).astype(BF16))
    want = lax.broadcasted_iota(jnp.int32, (MOST, tok), 0).astype(F32)
    picks = []
    scaled = []
    for k in range(n_e):
        hit = jnp.where(want == slot[k : k + 1], chosen[k], 0.0)
        picks.append(hit)
        scaled.append(hit * weight[k])
    picks = jnp.concatenate(picks, axis=0).astype(BF16)
    scaled = jnp.concatenate(scaled, axis=0).astype(BF16)
    select[...] = picks
    for copy in fetch:
        copy.wait()
    for side, position in itertools.product(range(2), range(n_f // 2)):
        at = pl.ds(pl.multiple_of(slice_of(f, side, position, n_f) * width, width), width)
        here = slice(position * width, (position + 1) * width)
        x = mm(picks, tokens[:, at]).astype(BF16)
        q = mm(scaled, grads[:, at]).astype(BF16)
        for k in range(n_e):
            sends[k][side, :MOST, here] = x[k * MOST : (k + 1) * MOST]
            sends[k][side, MOST:, here] = q[k * MOST : (k + 1) * MOST]


def pack_kernel(*refs, n_e):
    sides = refs[:n_e], refs[n_e : 2 * n_e]
    outs = refs[2 * n_e :]
    width = outs[0].shape[2]
    rows = n_e * MOST
    for i, out in enumerate(outs):
        here = slice((i + 1) * width, (i + 2) * width)
        for side in range(2):
            for k in range(n_e):
                out[side, k * MOST : (k + 1) * MOST] = sides[side][k][side, :MOST, here]
                out[side, rows + k * MOST : rows + (k + 1) * MOST] = sides[side][k][side, MOST:, here]


def forward_kernel(*refs, n_e, entries, carried):
    sides = refs[:n_e], refs[n_e : 2 * n_e]
    refs = refs[2 * n_e :]
    if carried:
        total_in, refs = refs[0], refs[1:]
    count = len(entries)
    pieces, outs = refs[:count], refs[count:]
    width, hidden = pieces[0].shape[0] // 3, pieces[0].shape[1]

    def rows_of(part):
        return jnp.concatenate(
            [
                jnp.concatenate([sides[side][k][side, part, i * width : (i + 1) * width] for i in entries], axis=1)
                for side in range(2)
                for k in range(n_e)
            ],
            axis=0,
        )

    x, q = rows_of(slice(0, MOST)), rows_of(slice(MOST, 2 * MOST))
    rows = n_e * MOST
    for at, left in enumerate((x, x, q)):
        right = jnp.concatenate([p[at * width : (at + 1) * width] for p in pieces], axis=0)
        here = slice(at * hidden, (at + 1) * hidden)
        part = mm(left, right)
        if carried:
            part = part + total_in[:, here]
            outs[0][:, here] = part[:rows]
            outs[1][:, here] = part[rows:].astype(BF16)
        else:
            outs[0][:, here] = part


def delta_kernel(own, got, deltas, pick_out):
    hidden = own.shape[1] // 3
    a, b, r = (
        own[:, at * hidden : (at + 1) * hidden] + got[:, at * hidden : (at + 1) * hidden].astype(F32) for at in range(3)
    )
    s = jax.nn.sigmoid(a)
    silu = a * s
    h = (silu * b).astype(BF16)
    pick = jnp.sum(h.astype(F32) * r, axis=1, keepdims=True)
    deltas[:, :hidden] = (r * b * s * (1.0 + a * (1.0 - s))).astype(BF16)
    deltas[:, hidden : 2 * hidden] = (r * silu).astype(BF16)
    deltas[:, 2 * hidden :] = h
    coarse = pick.astype(BF16)
    fine = (pick - coarse.astype(F32)).astype(BF16)
    wide = pick_out.shape
    lane = lax.broadcasted_iota(jnp.int32, wide, 1)
    pick_out[...] = jnp.where(
        lane < wide[1] // 2, jnp.broadcast_to(coarse.astype(F32), wide), jnp.broadcast_to(fine.astype(F32), wide)
    ).astype(BF16)


def back_kernel(deltas, deltas_other, pick, *refs, n, n_e):
    pieces, outs = refs[:n], refs[n:]
    width, hidden = pieces[0].shape[0] // 3, pieces[0].shape[1]
    da = jnp.concatenate([deltas[:, :hidden], deltas_other[:, :hidden]], axis=0)
    du = jnp.concatenate([deltas[:, hidden : 2 * hidden], deltas_other[:, hidden : 2 * hidden]], axis=0)
    for i in range(n):
        c = (mm_trail(da, pieces[i][:width]) + mm_trail(du, pieces[i][width : 2 * width])).astype(BF16)
        here = slice(i * width, (i + 1) * width)
        for side in range(2):
            for k in range(n_e):
                at = (side * n_e + k) * MOST
                outs[k][side, :, here] = c[at : at + MOST]
    for side in range(2):
        for k in range(n_e):
            outs[k][side, :, n * width :] = pick[k * MOST : (k + 1) * MOST]


def weight_kernel(*refs, n_e, count, entries, carried):
    if 0 in entries:
        sides, refs = (refs[:n_e], refs[n_e : 2 * n_e]), refs[2 * n_e :]
    if carried:
        total_in, refs = refs[0], refs[1:]
    far = [i for i in entries if i]
    got, deltas = refs[: len(far)], refs[len(far) : len(far) + 2 * len(entries)]
    outs = refs[len(far) + 2 * len(entries) :]
    hidden = deltas[0].shape[1] // 3
    rows = n_e * MOST

    def rows_of(part):
        lefts = []
        for i in entries:
            for side in range(2):
                if i:
                    lefts.append(got[far.index(i)][side, part * rows : (part + 1) * rows])
                else:
                    width = sides[0][0].shape[2] // count
                    lefts += [s[side, part * MOST : (part + 1) * MOST, :width] for s in sides[side]]
        return jnp.concatenate(lefts, axis=0)

    x, q = rows_of(0), rows_of(1)
    for at, left in enumerate((x, x, q)):
        here = slice(at * hidden, (at + 1) * hidden)
        part = mm_lead(left, jnp.concatenate([d[:, here] for d in deltas], axis=0))
        if carried:
            outs[at][...] = (total_in[:, here] + part).astype(BF16)
        else:
            outs[0][:, here] = part


def final_kernel(pos, ids, gates, select, *refs, n_f, n_e):
    mine, other, (in_grad, gate_grad) = refs[:n_e], refs[n_e : 2 * n_e], refs[2 * n_e :]
    f, e = pos[0], pos[1]
    width = in_grad.shape[1] // n_f
    total = n_f // 2 * width
    for side in range(2):
        c = jnp.concatenate([(mine, other)[side][k][side, :, :total] for k in range(n_e)], axis=0)
        rows = mm_lead(select[...], c).astype(BF16)
        for position in range(n_f // 2):
            at = pl.ds(pl.multiple_of(slice_of(f, side, position, n_f) * width, width), width)
            in_grad[:, at] = rows[:, position * width : (position + 1) * width]
    half = (mine[0].shape[2] - total) // 2
    found = jnp.zeros(ids.shape, F32)
    for k in range(n_e):
        pick = mine[k][0, :, total : total + 1].astype(F32) + mine[k][0, :, total + half : total + half + 1].astype(F32)
        hit = select[k * MOST : (k + 1) * MOST].astype(F32)
        value = jnp.sum(hit * pick, axis=0, keepdims=True)
        found = found + jnp.where(ids[...] == (e ^ k), value, 0.0)
    gate_grad[...] = (found / gates[...].astype(F32)).astype(BF16)


def call(kernel, args, places, outs, mib, scratch=(), places_out=None, hint=False, **static):
    args = [pltpu.with_memory_space_constraint(x, pltpu.HBM) if p == "h" else x for x, p in zip(args, places)]
    spaces = {"s": pltpu.SMEM, "v": pltpu.VMEM, "a": pl.ANY, "h": pltpu.HBM}
    return pl.pallas_call(
        functools.partial(kernel, **static),
        out_shape=outs,
        in_specs=[pl.BlockSpec(memory_space=spaces[p]) for p in places],
        **({"out_specs": pl.BlockSpec(memory_space=spaces[places_out])} if places_out else {}),
        scratch_shapes=scratch,
        **({"cost_estimate": HINT} if hint else {}),
        compiler_params=pltpu.CompilerParams(vmem_limit_bytes=mib * MIB),
    )(*args)


def after(x, *needs):
    return lax.optimization_barrier((x, *needs))[0] if needs else x


def to(x, position):
    n_f = lax.axis_size("fsdp")
    bits = n_f.bit_length() - 2
    return lax.ppermute(x, "fsdp", [(i, i ^ flips(position, i & 1, bits)) for i in range(n_f)])


def top(position):
    return 1 << (position.bit_length() - 1)


def per_device(tokens, out_grad, expert_ids, gate_probs, w_gate, w_up, w_down):
    tok, model = tokens.shape
    local, _, hidden = w_gate.shape
    n_f, n_e = lax.axis_size("fsdp"), lax.axis_size("ep")
    rows = n_e * MOST
    n = n_f // 2
    bits = n.bit_length() - 1
    near = [1 << b for b in range(bits)]
    late = [p for p in range(1, n) if p not in near]
    early = [0, *near]
    shape = jax.ShapeDtypeStruct

    weights = {
        0: call(
            stack_kernel,
            (w_gate[:, 0], w_up[:, 0], w_down[:, 0]),
            "hhh",
            shape((3 * local, hidden), BF16),
            8,
            [pltpu.SemaphoreType.DMA((3,))],
            places_out="a",
        )
    }
    for p in near:
        weights[p] = to(weights[0], p)

    pos = jnp.stack([lax.axis_index("fsdp"), lax.axis_index("ep")]).astype(jnp.int32)
    ids, gates = expert_ids.T, gate_probs.T
    *sends, select = call(
        prep_kernel,
        (pos, ids, gates, tokens, out_grad),
        "svvhh",
        [shape((2, 2 * MOST, model // 2), BF16)] * n_e + [shape((rows, tok), BF16)],
        16,
        [pltpu.VMEM(tokens.shape, BF16)] * 2 + [pltpu.SemaphoreType.DMA((2,))],
        n_f=n_f,
        n_e=n_e,
    )
    mine = [sends[0]] + [hop(sends[k], "ep", k) for k in range(1, n_e)]
    other = [hop(after(mine[0], weights[near[-1]]), "fsdp", 1)] + [hop(m, "fsdp", 1) for m in mine[1:]]
    both = (*mine, *other)
    for p in late:
        weights[p] = to(after(weights[p ^ top(p)], mine[1]), top(p))

    packed = call(pack_kernel, both, "v" * 2 * n_e, [shape((2, 2 * rows, local), BF16)] * (n - 1), 16, hint=True, n_e=n_e)
    got = [to(x, i + 1) for i, x in enumerate(packed)]

    def forward(entries, carried):
        pieces = [weights[p] for p in entries]
        return call(
            forward_kernel,
            (*both, *carried, *pieces),
            "v" * (2 * n_e + len(carried) + len(pieces)),
            [shape((rows, 3 * hidden), F32), shape((rows, 3 * hidden), BF16)]
            if carried
            else [shape((2 * rows, 3 * hidden), F32)],
            32,
            n_e=n_e,
            entries=entries,
            carried=bool(carried),
        )

    part = forward(early, ())[0]
    own, theirs = forward(late, [after(part, got[0])])
    deltas0, pick = call(
        delta_kernel, (own, hop(theirs, "fsdp", 1)), "vv", [shape((rows, 3 * hidden), BF16), shape((rows, 128), BF16)], 16
    )
    deltas = {0: deltas0}
    for p in near:
        deltas[p] = to(deltas0, p)
    deltas_other = {0: hop(deltas0, "fsdp", 1)}

    backs = call(
        back_kernel,
        (deltas[0], deltas_other[0], pick, *(weights[p] for p in range(n))),
        "v" * (3 + n),
        [shape((2, MOST, model // 2 + 128), BF16)] * n_e,
        24,
        n=n,
        n_e=n_e,
    )
    back = [backs[0]] + [hop(backs[k], "ep", k) for k in range(1, n_e)]
    for p in late:
        deltas[p] = to(after(deltas[p ^ top(p)], back[1], *got[1:-1]), top(p))
    for p in near:
        deltas_other[p] = hop(after(deltas[p], *back[1:4:2]), "fsdp", 1)

    def weight_sums(entries, carried):
        far = [got[p - 1] for p in entries if p]
        parts = [x for p in entries for x in (deltas[p], deltas_other[mirror(p, bits)])]
        here = both if 0 in entries else ()
        return call(
            weight_kernel,
            (*here, *carried, *far, *parts),
            "v" * (len(here) + len(carried) + len(far) + len(parts)),
            [shape((local, hidden), BF16)] * 3 if carried else [shape((local, 3 * hidden), F32)],
            32,
            count=n,
            n_e=n_e,
            entries=entries,
            carried=bool(carried),
        )

    part = weight_sums(early, ())[0]
    back_other = [hop(after(x, part) if k == 2 % n_e else x, "fsdp", 1) for k, x in enumerate(back)]
    in_grad, gate_grad = call(
        final_kernel,
        (pos, ids, gates, select, *back, *back_other),
        "svvv" + "v" * 2 * n_e,
        [shape((tok, model), BF16), shape(ids.shape, BF16)],
        16,
        n_f=n_f,
        n_e=n_e,
    )

    for p in late:
        deltas_other[p] = hop(after(deltas[p], part, in_grad, got[-1]), "fsdp", 1)
    grads = weight_sums(late, [part])
    return (in_grad, gate_grad.T, *(g[:, None] for g in grads))


def solution(mesh):
    tok = P(("fsdp", "ep"), None)
    weight = P("fsdp", "ep", None)
    return jax.shard_map(
        per_device,
        mesh=mesh,
        in_specs=(tok, tok, tok, tok, weight, weight, weight),
        out_specs=(tok, tok, weight, weight, weight),
        check_vma=False,
    )
```
